256 devices in a mesh: tm: 16 (over y_lo, x, core), blk: 8 (over z), samp: 2 (over y_hi).
Axes of the slice: x: 4, y: 4 (y_hi: 2, y_lo: 2; y = y_hi * 2 + y_lo), z: 8, core: 2. Of those that a mesh axis runs over, the one named last changes fastest.
Arguments:
- prior_path: float32 [32, 16, 1024], P('tm', 'samp', 'blk'), may hold values from -6 to 6
- observed: float32 [32, 256], P('tm', 'blk'), may hold values from -6 to 6
- obs_mask: int32 [32, 32], P('tm', 'blk'), may hold values 0 or 1
- noise_draw: float32 [32, 16, 256], P('tm', 'samp', 'blk'), may hold values from -6 to 6
- wend_blocks: float32 [128, 8, 8], P('blk'), may hold values from -1 to 1
- block_cols: int32 [128], P('blk'), may hold values from 0 to 31, as said below
- start_mean: float32 [16, 1024], P('samp', 'blk'), may hold values from -6 to 6
- trans_mats: bfloat16 [32, 1024, 1024], P('tm', 'blk', 'samp')
- gain_mats: bfloat16 [32, 1024, 256], P('tm', 'blk', 'samp'), may hold values from -0.375 to 0.375
- smooth_mats: bfloat16 [32, 1024, 1024], P('tm', 'blk', 'samp')
- site_trans: float32 [4, 4], replicated, may hold values from -2.5 to 2.5
Outputs:
- posterior_path: float32 [32, 16, 1024], P('tm', 'samp', 'blk')
The draws below stay inside these ranges and needn't reach their ends.
Inputs may be any that keep to these rules, and one draw needn't show every extreme that they name: `block_cols`: entry 4 i names block i itself, entries 4 i + 1 to 4 i + 3 name three different blocks among i - 2, i - 1, i + 1, i + 2 taken modulo 32.
All inputs are finite; a program needn't handle non-finite values. No bound on the sum of `obs_mask` on one device may be relied on, other than what follows from the above.
Results may differ from the reference program's by a relative error of at most 0.0003.
Values may be sent and summed in bfloat16 or wider, within the bound.
No kernel may reach another device: no remote copies, remote signals or barrier semaphores. Data moves between devices by JAX's collectives and lax.ppermute only.
A program may use at most 64 MiB of HBM per device.

```python
import math
import jax
import jax.numpy as jnp
from jax import lax

SITES = 256
SBLK = 8
T_DEV = 2
NSTATE = 1024
NBLOCKS = 32
PAIRS = 128
TIMES = 32
SAMPLES = 16
N_TM = 16


def decaying_steps(key):
    falloff_key, spike_key, noise_key = jax.random.split(key, 3)
    width_all = 4 * SITES
    total_steps = T_DEV * N_TM
    rate_low, rate_high = (0.01, 0.5)
    falloff_rates = jnp.exp(jax.random.uniform(falloff_key, (width_all,), jnp.float32, math.log(rate_low), math.log(rate_high)))
    spike_multiplier = jnp.where(jax.random.randint(spike_key, (total_steps, 1), 0, 12) == 0, 0.6, 1.0)
    main_diagonal = jnp.exp(-falloff_rates)[None, :] * spike_multiplier
    random_part = jax.random.normal(noise_key, (total_steps, width_all, width_all), jnp.float32) * (0.2 / math.sqrt(width_all))
    identity = jnp.eye(width_all, dtype=jnp.float32)
    return (random_part + main_diagonal[:, :, None] * identity[None, :, :]).astype(jnp.bfloat16)


def draw_trans_mats(key, part):
    return decaying_steps(jax.random.fold_in(key, 11))


def draw_smooth_mats(key, part):
    return decaying_steps(jax.random.fold_in(key, 23))


def draw_block_cols(key, part):
    block_count = SITES // SBLK
    scores = jax.random.randint(jax.random.fold_in(key, 5), (block_count, 4), 0, 4096) * 4 + jnp.arange(4, dtype=jnp.int32)[None, :]
    ranking = jnp.argsort(scores, axis=1)
    candidates = jnp.array([-2, -1, 1, 2], dtype=jnp.int32)
    picked = candidates[ranking[:, :3]]
    offsets = jnp.concatenate([jnp.zeros((block_count, 1), jnp.int32), picked], axis=1)
    return ((jnp.arange(block_count, dtype=jnp.int32)[:, None] + offsets) % block_count).reshape(-1).astype(jnp.int32)


def place_ends(result, rng, low, top_value):
    spot = [jax.random.randint(jax.random.fold_in(rng, axis), (), 0, length) for axis, length in enumerate(result.shape)]
    main_axis = result.shape.index(max(result.shape))
    beside = spot[:main_axis] + [(spot[main_axis] + 1) % result.shape[main_axis]] + spot[main_axis + 1:]
    return result.at[tuple(spot)].set(low).at[tuple(beside)].set(top_value)


def block_levels(key, dims, shards, least, largest):
    def one(axis_at, parts):
        draws = jax.random.uniform(jax.random.fold_in(jax.random.fold_in(key, 6), axis_at), (parts,), jnp.float32, least / len(shards), largest / len(shards))
        return jnp.repeat(jnp.exp(draws), dims[axis_at] // parts).reshape((-1,) + (1,) * (len(dims) - axis_at - 1))

    loudness = one(*shards[0])
    for cut in shards[1:]:
        loudness = loudness * one(*cut)
    return loudness


def noise(rng, shape, deviation, reach, cuts=(), held_as=jnp.bfloat16):
    values = deviation * jax.random.normal(rng, shape, jnp.float32)
    if cuts:
        values = values * block_levels(rng, shape, cuts, -0.22, 0.18)
    return jnp.clip(values, -reach, reach).astype(held_as)


def setup_inputs(seed: int = 0) -> dict:
    streams_of = jax.random.split(jax.random.key(seed), 12)
    prior_path = noise(streams_of[0], (TIMES, SAMPLES, NSTATE), 1.0, 6.0, ((0, 16), (1, 2), (2, 8)), jnp.float32)
    observed = noise(streams_of[1], (TIMES, SITES), 1.0, 6.0, ((0, 16), (1, 8)), jnp.float32)
    obs_mask = place_ends((jax.random.randint(streams_of[2], (TIMES, NBLOCKS), 0, 4) < 3).astype(jnp.int32), jax.random.fold_in(streams_of[2], 1), 0, 1)
    noise_draw = noise(streams_of[3], (TIMES, SAMPLES, SITES), 1.0, 6.0, ((0, 16), (1, 2), (2, 8)), jnp.float32)
    wend_blocks = noise(streams_of[4], (PAIRS, SBLK, SBLK), (4 * SBLK) ** -0.5, 1.0, ((0, 8),), jnp.float32)
    block_cols = draw_block_cols(jax.random.fold_in(streams_of[11], 71), 0)
    start_mean = noise(streams_of[6], (SAMPLES, NSTATE), 1.0, 6.0, ((0, 2), (1, 8)), jnp.float32)
    trans_mats = draw_trans_mats(jax.random.fold_in(streams_of[11], 71), 0)
    gain_mats = noise(streams_of[8], (TIMES, NSTATE, SITES), SITES ** -0.5, 0.375, ((0, 16), (1, 8), (2, 2)))
    smooth_mats = draw_smooth_mats(jax.random.fold_in(streams_of[11], 71), 0)
    site_trans = noise(streams_of[10], (4, 4), 0.5, 2.5, (), jnp.float32)
    return {"prior_path": prior_path, "observed": observed, "obs_mask": obs_mask, "noise_draw": noise_draw, "wend_blocks": wend_blocks, "block_cols": block_cols, "start_mean": start_mean, "trans_mats": trans_mats, "gain_mats": gain_mats, "smooth_mats": smooth_mats, "site_trans": site_trans}


highest = lax.Precision.HIGHEST


def reference(prior_path, observed, obs_mask, noise_draw, wend_blocks, block_cols, start_mean, trans_mats, gain_mats, smooth_mats, site_trans):
    block_count = SITES // SBLK
    noise_cells = noise_draw.reshape(TIMES, SAMPLES, block_count, SBLK)
    picked = noise_cells[:, :, block_cols, :]
    mixed = jnp.einsum('tspj,pij->tspi', picked, wend_blocks, precision=highest)
    obs_noise = jnp.sum(mixed.reshape(TIMES, SAMPLES, block_count, 4, SBLK), axis=3).reshape(TIMES, SAMPLES, SITES)
    first_comp = prior_path.reshape(TIMES, SAMPLES, SITES, 4)[:, :, :, 0]
    seen_mask = jnp.repeat(obs_mask.astype(jnp.float32), SBLK, axis=1)
    residual = seen_mask[:, None, :] * (observed[:, None, :] - first_comp - obs_noise)

    def forward_step(state, step_inputs):
        trans_step, gain_step, resid_step = step_inputs
        pushed = jnp.einsum('ij,sj->si', trans_step.astype(jnp.float32), state, precision=highest)
        added = jnp.einsum('ij,sj->si', gain_step.astype(jnp.float32), resid_step, precision=highest)
        state = pushed + added
        return state, state

    final_carry, filtered = lax.scan(forward_step, start_mean, (trans_mats, gain_mats, residual))
    site_kron = jnp.kron(jnp.eye(SITES, dtype=jnp.float32), site_trans)
    predicted = jnp.einsum('ij,tsj->tsi', site_kron, filtered, precision=highest)

    def backward_step(next_state, step_inputs):
        smooth_step, filt_step, pred_step = step_inputs
        state = filt_step + jnp.einsum('ij,sj->si', smooth_step.astype(jnp.float32), next_state - pred_step, precision=highest)
        return state, state

    final_state = filtered[-1]
    back_carry, smoothed_head = lax.scan(backward_step, final_state, (smooth_mats[:-1], filtered[:-1], predicted[:-1]), reverse=True)
    smoothed = jnp.concatenate([smoothed_head, final_state[None]], axis=0)
    return prior_path + smoothed
```

```python
import functools
import jax
import jax.numpy as jnp
from jax import lax
from jax.experimental import pallas as pl
from jax.experimental.pallas import tpu as pltpu
from jax.sharding import PartitionSpec as P

highest = lax.Precision.HIGHEST
bf16, f32 = jnp.bfloat16, jnp.float32
ROWS_BY_ROWS = (((1,), (1,)), ((), ()))
VMEM_LIMIT = 8 * 1024 * 1024


def ring(count, step):
    return [(i, (i + step) % count) for i in range(count)]


def swapped(count):
    return [(i, i ^ 1) for i in range(count)]


def all_blocks(value, axis):
    count = lax.axis_size(axis)
    copies = jnp.broadcast_to(value[None], (count,) + value.shape)
    return lax.all_to_all(copies, axis, 0, 0, tiled=True)


def observation_noise(noise_draw, wend_blocks, block_cols):
    step_count, sample_count, local_sites = noise_draw.shape
    block_sites = wend_blocks.shape[1]
    local_blocks = local_sites // block_sites
    cycle = lax.axis_size("blk")
    rim = 2 * block_sites
    before = lax.ppermute(noise_draw[:, :, local_sites - rim :], "blk", ring(cycle, 1))
    after = lax.ppermute(noise_draw[:, :, :rim], "blk", ring(cycle, -1))
    widened = jnp.concatenate([before, noise_draw, after], axis=2)
    pair_rows = jnp.arange(local_blocks * 4, dtype=jnp.int32) // 4
    first_block = lax.axis_index("blk") * local_blocks
    offset = (block_cols - first_block - pair_rows + 2) % (local_blocks * cycle)
    chooser = (
        (pair_rows + offset)[:, None] == jnp.arange(local_blocks + 4, dtype=jnp.int32)[None, :]
    ).astype(f32)
    blocks = wend_blocks.reshape(local_blocks, 4, block_sites, block_sites)
    chooser = chooser.reshape(local_blocks, 4, local_blocks + 4)
    mixer = jnp.sum(chooser[:, :, :, None, None] * blocks[:, :, None, :, :], axis=1)
    mixer = mixer.transpose(1, 3, 0, 2).reshape(local_sites + 2 * rim, local_sites)
    return jnp.einsum("tsl,lm->tsm", widened, mixer, precision=highest)


def split_rows(value):
    high = value.astype(bf16)
    rest = value - high.astype(f32)
    middle = rest.astype(bf16)
    low = (rest - middle.astype(f32)).astype(bf16)
    return jnp.concatenate([high, middle, low], axis=0)


def joined_rows(value):
    rows = value.shape[0] // 3
    return value[:rows] + value[rows : 2 * rows] + value[2 * rows :]


def halves_of(split_ref, samp):
    width = split_ref.shape[1] // 2
    mine = split_ref[:, pl.ds(pl.multiple_of(samp * width, 128), width)]
    other = split_ref[:, pl.ds(pl.multiple_of((1 - samp) * width, 128), width)]
    return mine, other


def forward_kernel(count, place, state_ref, near_in, far_in, *refs):
    near = (refs[:count], refs[count : 2 * count])
    far = (refs[2 * count : 3 * count], refs[3 * count : 4 * count])
    out_ref, split_ref = refs[4 * count :]
    blk, samp, core = place[0], place[1], place[2]

    def run(order):
        for turn in range(4):
            shards, inputs = order[turn // 2]
            step = turn % 2
            state = state_ref[...] if turn == 0 else out_ref[turn - 1]
            split_ref[...] = split_rows(state)
            mine, other = halves_of(split_ref, samp)
            for k in range(0, count, 2):
                first = jnp.concatenate([shards[0][k][step], shards[0][k + 1][step]], axis=0)
                second = jnp.concatenate([shards[1][k][step], shards[1][k + 1][step]], axis=0)
                part = joined_rows(
                    lax.dot_general(mine, first, ROWS_BY_ROWS, preferred_element_type=f32)
                    + lax.dot_general(other, second, ROWS_BY_ROWS, preferred_element_type=f32)
                )
                width = part.shape[1] // 2
                for q in range(2):
                    at = lax.rem(blk - (k + q) + count, count)
                    columns = pl.ds(pl.multiple_of(at * width, 128), width)
                    out_ref[turn, :, columns] = (
                        part[:, q * width : (q + 1) * width] + inputs[step, :, columns]
                    )

    @pl.when(core == 0)
    def _():
        run(((near, near_in), (far, far_in)))

    @pl.when(core == 1)
    def _():
        run(((far, far_in), (near, near_in)))


def backward_kernel(place, state_ref, filt_ref, pred_ref, near, far, out_ref, split_ref):
    samp, core, is_last = place[1], place[2], place[3]
    count = near.shape[0]

    def run(order):
        for turn in range(3, -1, -1):
            mats = order[turn // 2]
            step = turn % 2
            later = state_ref[...] if turn == 3 else out_ref[turn + 1]
            split_ref[...] = split_rows(later - pred_ref[turn])
            mine, other = halves_of(split_ref, samp)
            for k in range(0, count, 2):
                first = jnp.concatenate([mats[k, 0, step], mats[k + 1, 0, step]], axis=0)
                second = jnp.concatenate([mats[k, 1, step], mats[k + 1, 1, step]], axis=0)
                part = joined_rows(
                    lax.dot_general(mine, first, ROWS_BY_ROWS, preferred_element_type=f32)
                    + lax.dot_general(other, second, ROWS_BY_ROWS, preferred_element_type=f32)
                )
                if turn == 3:
                    part = jnp.where(is_last == 1, 0.0, part)
                width = part.shape[1]
                columns = pl.ds(k * (width // 2), width)
                out_ref[turn, :, columns] = filt_ref[turn, :, columns] + part

    @pl.when(core == 0)
    def _():
        run((near, far))

    @pl.when(core == 1)
    def _():
        run((far, near))


def predict_kernel(filt_ref, kron_ref, out_ref):
    steps, samples, states = filt_ref.shape
    width = kron_ref.shape[0]
    for k in range(0, states, width):
        rows = filt_ref[:, :, k : k + width].reshape(steps * samples, width)
        moved = lax.dot_general(
            rows, kron_ref[...], ROWS_BY_ROWS, precision=highest, preferred_element_type=f32
        )
        out_ref[:, :, k : k + width] = moved.reshape(steps, samples, width)


def call(kernel, name, shape, scalars, vectors, split):
    specs = [pl.BlockSpec(memory_space=pltpu.SMEM)] * scalars
    specs += [pl.BlockSpec(memory_space=pltpu.VMEM)] * vectors
    return pl.pallas_call(
        kernel,
        out_shape=jax.ShapeDtypeStruct(shape, f32),
        in_specs=specs,
        out_specs=pl.BlockSpec(memory_space=pltpu.VMEM),
        scratch_shapes=[pltpu.VMEM((3 * shape[1], shape[2]), bf16)] if split else [],
        compiler_params=pltpu.CompilerParams(vmem_limit_bytes=VMEM_LIMIT),
        name=name,
    )


def in_vmem(value):
    return pltpu.with_memory_space_constraint(value, pltpu.VMEM)


def on_device(
    prior_path,
    observed,
    obs_mask,
    noise_draw,
    wend_blocks,
    block_cols,
    start_mean,
    trans_mats,
    gain_mats,
    smooth_mats,
    site_trans,
):
    cycle, times = lax.axis_size("blk"), lax.axis_size("tm")
    blk, samp, time = lax.axis_index("blk"), lax.axis_index("samp"), lax.axis_index("tm")
    groups = times // 2
    group, core = time // 2, time % 2
    step_count, sample_count, local_sites = noise_draw.shape
    block_sites = wend_blocks.shape[1]
    state_count = trans_mats.shape[1] * cycle
    cores = swapped(times)
    place = jnp.stack([blk, samp, core, (group == groups - 1).astype(jnp.int32)]).astype(jnp.int32)

    mine = trans_mats
    other = lax.ppermute(trans_mats, "samp", swapped(2))
    near_mine, near_other = [None] * cycle, [None] * cycle
    near_mine[0], near_other[0] = mine, other
    half = cycle // 2
    for k in range(1, half + 1):
        near_mine[k] = lax.ppermute(near_mine[k - 1], "blk", ring(cycle, 1))
        if k < half:
            near_mine[cycle - k] = lax.ppermute(
                near_mine[(cycle - k + 1) % cycle], "blk", ring(cycle, -1)
            )
            near_other[k] = lax.ppermute(near_other[k - 1], "blk", ring(cycle, 1))
        near_other[cycle - k] = lax.ppermute(
            near_other[(cycle - k + 1) % cycle], "blk", ring(cycle, -1)
        )
    far_mine = [lax.ppermute(v, "tm", cores) for v in near_mine]
    far_other = [lax.ppermute(v, "tm", cores) for v in near_other]
    shards = [in_vmem(v) for v in near_mine + near_other + far_mine + far_other]

    obs_noise = observation_noise(noise_draw, wend_blocks, block_cols)
    first_comp = prior_path.reshape(step_count, sample_count, local_sites, 4)[:, :, :, 0]
    seen_mask = jnp.repeat(obs_mask.astype(f32), block_sites, axis=1)
    residual = seen_mask[:, None, :] * (observed[:, None, :] - first_comp - obs_noise)
    all_resid = all_blocks(residual, "blk").transpose(1, 2, 0, 3)
    all_resid = all_resid.reshape(step_count, sample_count, local_sites * cycle)
    gain_other = lax.ppermute(gain_mats, "samp", swapped(2))
    gain = jnp.where(
        samp == 0,
        jnp.concatenate([gain_mats, gain_other], axis=2),
        jnp.concatenate([gain_other, gain_mats], axis=2),
    )
    inputs = jnp.einsum("tij,tsj->tsi", gain, all_resid, precision=highest)
    gathered = all_blocks(jnp.concatenate([inputs, start_mean[None]], axis=0), "blk")
    gathered = gathered.transpose(1, 2, 0, 3).reshape(step_count + 1, sample_count, state_count)
    near_in, start = gathered[:step_count], gathered[step_count]
    far_in = lax.ppermute(near_in, "tm", cores)

    smooth_other = lax.ppermute(smooth_mats, "samp", swapped(2))
    near_smooth = lax.all_gather(jnp.stack([smooth_mats, smooth_other]), "blk", axis=0)
    far_smooth = lax.ppermute(near_smooth, "tm", cores)
    near_smooth, far_smooth = in_vmem(near_smooth), in_vmem(far_smooth)

    shape = (4, sample_count, state_count)
    forward = call(
        functools.partial(forward_kernel, cycle), "forward", shape, 1, 3 + 4 * cycle, True
    )
    state = jnp.where(group == 0, start, 0.0)
    for hop in range(groups - 1):
        filtered = forward(place, state, near_in, far_in, *shards)
        sent = [(2 * hop, 2 * hop + 2), (2 * hop + 1, 2 * hop + 3)]
        received = lax.ppermute(filtered[3], "tm", sent)
        state = jnp.where(group == hop + 1, received, state)
    filtered = forward(place, state, near_in, far_in, *shards)

    sites = 32
    kron = jnp.kron(jnp.eye(sites, dtype=f32), site_trans)
    predicted = call(predict_kernel, "predict", shape, 0, 2, False)(filtered, kron)
    backward = call(backward_kernel, "backward", shape, 1, 5, True)
    state = jnp.zeros((sample_count, state_count), f32)
    for hop in range(groups - 1):
        smoothed = backward(place, state, filtered, predicted, near_smooth, far_smooth)
        source = 2 * (groups - 1 - hop)
        received = lax.ppermute(
            smoothed[0], "tm", [(source, source - 2), (source + 1, source - 1)]
        )
        state = jnp.where(group == groups - 2 - hop, received, state)
    smoothed = backward(place, state, filtered, predicted, near_smooth, far_smooth)
    width = state_count // cycle
    mine = lax.dynamic_slice(
        smoothed, (2 * core, 0, blk * width), (step_count, sample_count, width)
    )
    return prior_path + mine


def solution(mesh):
    placed = (
        P("tm", "samp", "blk"),
        P("tm", "blk"),
        P("tm", "blk"),
        P("tm", "samp", "blk"),
        P("blk", None, None),
        P("blk"),
        P("samp", "blk"),
        P("tm", "blk", "samp"),
        P("tm", "blk", "samp"),
        P("tm", "blk", "samp"),
        P(),
    )
    return jax.shard_map(
        on_device, mesh=mesh, in_specs=placed, out_specs=P("tm", "samp", "blk"), check_vma=False
    )
```

```python
import functools
import jax
import jax.numpy as jnp
from jax import lax
from jax.experimental import pallas as pl
from jax.experimental.pallas import tpu as pltpu
from jax.sharding import PartitionSpec as P

highest = lax.Precision.HIGHEST
bf16, f32 = jnp.bfloat16, jnp.float32
ROWS_BY_ROWS = (((1,), (1,)), ((), ()))
VMEM_LIMIT = 2 * 1024 * 1024


def ring(count, step):
    return [(i, (i + step) % count) for i in range(count)]


def swapped(count):
    return [(i, i ^ 1) for i in range(count)]


def all_blocks(value, axis):
    count = lax.axis_size(axis)
    copies = jnp.broadcast_to(value[None], (count,) + value.shape)
    return lax.all_to_all(copies, axis, 0, 0, tiled=True)


def observation_noise(noise_draw, wend_blocks, block_cols):
    step_count, sample_count, local_sites = noise_draw.shape
    block_sites = wend_blocks.shape[1]
    local_blocks = local_sites // block_sites
    cycle = lax.axis_size("blk")
    rim = 2 * block_sites
    before = lax.ppermute(noise_draw[:, :, local_sites - rim :], "blk", ring(cycle, 1))
    after = lax.ppermute(noise_draw[:, :, :rim], "blk", ring(cycle, -1))
    widened = jnp.concatenate([before, noise_draw, after], axis=2)
    pair_rows = jnp.arange(local_blocks * 4, dtype=jnp.int32) // 4
    first_block = lax.axis_index("blk") * local_blocks
    offset = (block_cols - first_block - pair_rows + 2) % (local_blocks * cycle)
    chooser = (
        (pair_rows + offset)[:, None] == jnp.arange(local_blocks + 4, dtype=jnp.int32)[None, :]
    ).astype(f32)
    blocks = wend_blocks.reshape(local_blocks, 4, block_sites, block_sites)
    chooser = chooser.reshape(local_blocks, 4, local_blocks + 4)
    mixer = jnp.sum(chooser[:, :, :, None, None] * blocks[:, :, None, :, :], axis=1)
    mixer = mixer.transpose(1, 3, 0, 2).reshape(local_sites + 2 * rim, local_sites)
    return jnp.einsum("tsl,lm->tsm", widened, mixer, precision=highest)


def split_rows(value):
    high = value.astype(bf16)
    rest = value - high.astype(f32)
    middle = rest.astype(bf16)
    low = (rest - middle.astype(f32)).astype(bf16)
    return jnp.concatenate([high, middle, low], axis=0)


def joined_rows(value):
    rows = value.shape[0] // 3
    return value[:rows] + value[rows : 2 * rows] + value[2 * rows :]


def start_copies(shards, out_ref, sems, used, owner, side):
    width = shards.shape[3]
    columns = pl.ds(pl.multiple_of(side * width, 128), width)
    copies = []
    for step in range(shards.shape[1]):
        target = out_ref.at[owner * shards.shape[1] + step, :, :, columns]
        copy = pltpu.make_async_copy(shards.at[:, step], target, sems.at[used + step])
        copy.start()
        copies.append(copy)
    return copies


def pack_ring_kernel(count, place, near, far, *refs):
    shards, out_ref, sems = refs[: 2 * count], refs[2 * count], refs[2 * count + 1]
    blk, samp, core = place[0], place[1], place[2]
    copies = start_copies(near, out_ref, sems, 0, core, samp)
    copies += start_copies(far, out_ref, sems, 2, 1 - core, samp)
    for n, shard in enumerate(shards):
        whose, k = n // count, n % count
        steps, rows, width = shard.shape
        owner = core if whose == 0 else 1 - core
        at = lax.rem(blk - k + count, count)
        columns = pl.ds(pl.multiple_of((1 - samp) * width, 128), width)
        target = out_ref.at[pl.ds(owner * steps, steps), at, :, columns]
        copy = pltpu.make_async_copy(shard, target, sems.at[4 + n])
        copy.start()
        copies.append(copy)
    for copy in copies:
        copy.wait()


def pack_kernel(place, near, far, out_ref, sems):
    samp, core = place[1], place[2]
    copies = []
    for whose, shards in enumerate((near, far)):
        owner = core if whose == 0 else 1 - core
        for half in range(2):
            side = samp if half == 0 else 1 - samp
            copies += start_copies(shards.at[:, half], out_ref, sems, len(copies), owner, side)
    for copy in copies:
        copy.wait()


def apply_rows(mats, turn, value, store):
    count, rows, _ = mats.shape[1:]
    terms = split_rows(value)
    for k in range(0, count, 2):
        block = jnp.concatenate([mats[turn, k], mats[turn, k + 1]], axis=0)
        part = lax.dot_general(terms, block, ROWS_BY_ROWS, preferred_element_type=f32)
        store(slice(k * rows, (k + 2) * rows), joined_rows(part))


def forward_kernel(hop, place, state_ref, near_in, far_in, mats, *refs):
    filt_ref, sent_ref = refs[-2:]

    @pl.when(place[3] == hop)
    def _():
        sent_ref[...] = state_ref[...]

        def step(turn, carry):
            is_near = turn // 2 == place[2]

            def store(columns, part):
                at = lax.rem(turn, 2)
                added = jnp.where(is_near, near_in[at, :, columns], far_in[at, :, columns])
                filt_ref[turn, :, columns] = part + added

            apply_rows(mats, turn, sent_ref[...], store)
            sent_ref[...] = filt_ref[turn]
            return carry

        lax.fori_loop(0, 4, step, 0)


def backward_kernel(hop, hops, place, state_ref, filt_ref, pred_ref, mats, *refs):
    target_ref, sent_ref = refs[-2:]

    @pl.when(place[3] == hop)
    def _():
        sent_ref[...] = state_ref[...]

        def step(i, carry):
            turn = 3 - i
            change = sent_ref[...] - pred_ref[turn]
            if hop == hops - 1:
                change = jnp.where(turn == 3, 0.0, change)

            def store(columns, part):
                target_ref[turn, :, columns] = filt_ref[turn, :, columns] + part

            apply_rows(mats, turn, change, store)
            sent_ref[...] = target_ref[turn]
            return carry

        lax.fori_loop(0, 4, step, 0)


def finish_kernel(place, prior_ref, smooth_ref, out_ref):
    width = out_ref.shape[2]
    columns = pl.ds(pl.multiple_of(place[0] * width, 128), width)
    for step in range(2):
        out_ref[step] = prior_ref[step] + smooth_ref[place[2] * 2 + step, :, columns]


def predict_kernel(site_ref, filt_ref, out_ref):
    steps, samples, states = filt_ref.shape
    width = 128
    row = lax.broadcasted_iota(jnp.int32, (width, width), 0)
    column = lax.broadcasted_iota(jnp.int32, (width, width), 1)
    same_site = row // 4 == column // 4
    kron = jnp.zeros((width, width), f32)
    for i in range(4):
        for j in range(4):
            here = same_site & (row % 4 == i) & (column % 4 == j)
            kron = jnp.where(here, site_ref[i, j], kron)
    for k in range(0, states, width):
        rows = filt_ref[:, :, k : k + width].reshape(steps * samples, width)
        moved = lax.dot_general(
            rows, kron, ROWS_BY_ROWS, precision=highest, preferred_element_type=f32
        )
        out_ref[:, :, k : k + width] = moved.reshape(steps, samples, width)


SMEM = pl.BlockSpec(memory_space=pltpu.SMEM)
VMEM = pl.BlockSpec(memory_space=pltpu.VMEM)
ANY = pl.BlockSpec(memory_space=pl.ANY)
HBM = pl.BlockSpec(memory_space=pltpu.HBM)


def call(kernel, name, shapes, specs, scratch=(), aliases=None):
    return pl.pallas_call(
        kernel,
        out_shape=shapes,
        in_specs=specs,
        out_specs=jax.tree.map(lambda _: VMEM, shapes),
        scratch_shapes=list(scratch),
        input_output_aliases=aliases or {},
        compiler_params=pltpu.CompilerParams(vmem_limit_bytes=VMEM_LIMIT),
        name=name,
    )


def in_vmem(value):
    return pltpu.with_memory_space_constraint(value, pltpu.VMEM)


def on_device(
    prior_path,
    observed,
    obs_mask,
    noise_draw,
    wend_blocks,
    block_cols,
    start_mean,
    trans_mats,
    gain_mats,
    smooth_mats,
    site_trans,
):
    cycle, times = lax.axis_size("blk"), lax.axis_size("tm")
    blk, samp, time = lax.axis_index("blk"), lax.axis_index("samp"), lax.axis_index("tm")
    groups = times // 2
    group, core = time // 2, time % 2
    step_count, sample_count, local_sites = noise_draw.shape
    block_sites = wend_blocks.shape[1]
    state_count = trans_mats.shape[1] * cycle
    cores = swapped(times)
    place = jnp.stack([blk, samp, core, group]).astype(jnp.int32)

    trans_other = lax.ppermute(trans_mats, "samp", swapped(2))
    near = lax.all_gather(jnp.stack([trans_mats, trans_other]), "blk", axis=0)

    obs_noise = observation_noise(noise_draw, wend_blocks, block_cols)
    first_comp = prior_path.reshape(step_count, sample_count, local_sites, 4)[:, :, :, 0]
    seen_mask = jnp.repeat(obs_mask.astype(f32), block_sites, axis=1)
    residual = seen_mask[:, None, :] * (observed[:, None, :] - first_comp - obs_noise)
    all_resid = all_blocks(residual, "blk").transpose(1, 2, 0, 3)
    all_resid = all_resid.reshape(step_count, sample_count, local_sites * cycle)
    gain_other = lax.ppermute(gain_mats, "samp", swapped(2))
    gain = jnp.where(
        samp == 0,
        jnp.concatenate([gain_mats, gain_other], axis=2),
        jnp.concatenate([gain_other, gain_mats], axis=2),
    )
    inputs = jnp.einsum("tij,tsj->tsi", gain, all_resid, precision=highest)
    gathered = all_blocks(jnp.concatenate([inputs, start_mean[None]], axis=0), "blk")
    gathered = gathered.transpose(1, 2, 0, 3).reshape(step_count + 1, sample_count, state_count)
    near_in, start = gathered[:step_count], gathered[step_count]
    far_in = lax.ppermute(near_in, "tm", cores)
    mats_shape = jax.ShapeDtypeStruct((4, cycle, trans_mats.shape[1], state_count), bf16)

    def pack(value, name):
        far = lax.ppermute(value, "tm", cores)
        dmas = [pltpu.SemaphoreType.DMA((8,))]
        return in_vmem(call(pack_kernel, name, mats_shape, [SMEM, HBM, HBM], dmas)(place, value, far))

    near, near_in = lax.optimization_barrier((near, near_in))
    trans = pack(near, "pack_trans")

    smooth_mats, _ = lax.optimization_barrier((smooth_mats, all_resid))
    smooth_other = lax.ppermute(smooth_mats, "samp", swapped(2))
    near_smooth = lax.all_gather(jnp.stack([smooth_mats, smooth_other]), "blk", axis=0)

    filt_shape = jax.ShapeDtypeStruct((4, sample_count, state_count), f32)
    state_shape = jax.ShapeDtypeStruct((sample_count, state_count), f32)

    def forward(hop, state, *filtered):
        return call(
            functools.partial(forward_kernel, hop),
            "forward",
            (filt_shape, state_shape),
            [SMEM] + [VMEM] * (4 + len(filtered)),
            (),
            {5: 0} if filtered else None,
        )(place, state, near_in, far_in, trans, *filtered)

    filtered, sent = forward(0, start)
    for hop in range(1, groups):
        pairs = [(2 * hop - 2, 2 * hop), (2 * hop - 1, 2 * hop + 1)]
        state = lax.ppermute(sent, "tm", pairs)
        if hop == groups - 1:
            near_smooth, filtered = lax.optimization_barrier((near_smooth, filtered))
            smooth = pack(near_smooth, "pack_smooth")
            filtered, smooth = lax.optimization_barrier((filtered, smooth))
        filtered, sent = forward(hop, state, filtered)

    predicted = call(predict_kernel, "predict", filt_shape, [SMEM, VMEM])(site_trans, filtered)

    def backward(hop, state, *smoothed):
        return call(
            functools.partial(backward_kernel, hop, groups),
            "backward",
            (filt_shape, state_shape),
            [SMEM] + [VMEM] * (4 + len(smoothed)),
            (),
            {5: 0} if smoothed else None,
        )(place, state, filtered, predicted, smooth, *smoothed)

    smoothed, sent = backward(groups - 1, sent)
    for hop in range(groups - 2, -1, -1):
        pairs = [(2 * hop + 2, 2 * hop), (2 * hop + 3, 2 * hop + 1)]
        state = lax.ppermute(sent, "tm", pairs)
        smoothed, sent = backward(hop, state, smoothed)
    out_shape = jax.ShapeDtypeStruct(prior_path.shape, f32)
    return call(finish_kernel, "finish", out_shape, [SMEM, VMEM, VMEM])(place, prior_path, smoothed)


def solution(mesh):
    placed = (
        P("tm", "samp", "blk"),
        P("tm", "blk"),
        P("tm", "blk"),
        P("tm", "samp", "blk"),
        P("blk", None, None),
        P("blk"),
        P("samp", "blk"),
        P("tm", "blk", "samp"),
        P("tm", "blk", "samp"),
        P("tm", "blk", "samp"),
        P(),
    )
    return jax.shard_map(
        on_device, mesh=mesh, in_specs=placed, out_specs=P("tm", "samp", "blk"), check_vma=False
    )
```

```python
import functools
import jax
import jax.numpy as jnp
from jax import lax
from jax.experimental import pallas as pl
from jax.experimental.pallas import tpu as pltpu
from jax.sharding import PartitionSpec as P

highest = lax.Precision.HIGHEST
bf16, f32 = jnp.bfloat16, jnp.float32
ROWS_BY_ROWS = (((1,), (1,)), ((), ()))
VMEM_LIMIT = 2 * 1024 * 1024


def ring(count, step):
    return [(i, (i + step) % count) for i in range(count)]


def swapped(count):
    return [(i, i ^ 1) for i in range(count)]


def all_blocks(value, axis):
    count = lax.axis_size(axis)
    copies = jnp.broadcast_to(value[None], (count,) + value.shape)
    return lax.all_to_all(copies, axis, 0, 0, tiled=True)


def noise_rim(noise_draw, rim=16):
    cycle, local_sites = lax.axis_size("blk"), noise_draw.shape[2]
    before = lax.ppermute(noise_draw[:, :, local_sites - rim :], "blk", ring(cycle, 1))
    after = lax.ppermute(noise_draw[:, :, :rim], "blk", ring(cycle, -1))
    return jnp.concatenate([before, noise_draw, after], axis=2)


def noise_mixer(wend_blocks, block_cols):
    block_sites = wend_blocks.shape[1]
    local_blocks = block_cols.shape[0] // 4
    cycle = lax.axis_size("blk")
    pair_rows = jnp.arange(local_blocks * 4, dtype=jnp.int32) // 4
    first_block = lax.axis_index("blk") * local_blocks
    offset = (block_cols - first_block - pair_rows + 2) % (local_blocks * cycle)
    chooser = (
        (pair_rows + offset)[:, None] == jnp.arange(local_blocks + 4, dtype=jnp.int32)[None, :]
    ).astype(f32)
    blocks = wend_blocks.reshape(local_blocks, 4, block_sites, block_sites)
    chooser = chooser.reshape(local_blocks, 4, local_blocks + 4)
    mixer = jnp.sum(chooser[:, :, :, None, None] * blocks[:, :, None, :, :], axis=1)
    return mixer.transpose(1, 3, 0, 2).reshape(
        (local_blocks + 4) * block_sites, local_blocks * block_sites
    )


def split_rows(value):
    high = value.astype(bf16)
    low = (value - high.astype(f32)).astype(bf16)
    return jnp.concatenate([high, low], axis=0)


def joined_rows(value):
    rows = value.shape[0] // 2
    return value[:rows] + value[rows:]


def start_copies(shards, out_ref, sems, used, owner, side):
    width = shards.shape[3]
    columns = pl.ds(pl.multiple_of(side * width, 128), width)
    copies = []
    for step in range(shards.shape[1]):
        target = out_ref.at[owner * shards.shape[1] + step, :, :, columns]
        copy = pltpu.make_async_copy(shards.at[:, step], target, sems.at[used + step])
        copy.start()
        copies.append(copy)
    return copies


def pack_kernel(far, place, both, *refs):
    out_ref, sems = refs[-2:]
    samp, core = place[1], place[2]
    owner = 1 - core if far else core
    copies = start_copies(both.at[:, 0], out_ref, sems, 0, owner, samp)
    copies += start_copies(both.at[:, 1], out_ref, sems, 2, owner, 1 - samp)
    for copy in copies:
        copy.wait()


def apply_rows(mats, turn, value, store):
    count, rows, _ = mats.shape[1:]
    terms = split_rows(value)
    for k in range(0, count, 2):
        block = jnp.concatenate([mats[turn, k], mats[turn, k + 1]], axis=0)
        part = lax.dot_general(terms, block, ROWS_BY_ROWS, preferred_element_type=f32)
        store(slice(k * rows, (k + 2) * rows), joined_rows(part))


def forward_kernel(hop, place, state_ref, near_in, far_in, mats, *refs):
    filt_ref, sent_ref = refs[-2:]

    @pl.when(place[3] == hop)
    def _():
        sent_ref[...] = state_ref[...]

        def step(turn, carry):
            is_near = turn // 2 == place[2]

            def store(columns, part):
                at = lax.rem(turn, 2)
                added = jnp.where(is_near, near_in[at, :, columns], far_in[at, :, columns])
                filt_ref[turn, :, columns] = part + added

            apply_rows(mats, turn, sent_ref[...], store)
            sent_ref[...] = filt_ref[turn]
            return carry

        lax.fori_loop(0, 4, step, 0)


def backward_kernel(hop, hops, place, state_ref, filt_ref, pred_ref, mats, *refs):
    target_ref, sent_ref = refs[-2:]

    @pl.when(place[3] == hop)
    def _():
        sent_ref[...] = state_ref[...]

        def step(i, carry):
            turn = 3 - i
            change = sent_ref[...] - pred_ref[turn]
            if hop == hops - 1:
                change = jnp.where(turn == 3, 0.0, change)

            def store(columns, part):
                target_ref[turn, :, columns] = filt_ref[turn, :, columns] + part

            apply_rows(mats, turn, change, store)
            sent_ref[...] = target_ref[turn]
            return carry

        lax.fori_loop(0, 4, step, 0)


def finish_kernel(place, prior_ref, smooth_ref, out_ref):
    width = out_ref.shape[2]
    columns = pl.ds(pl.multiple_of(place[0] * width, 128), width)
    for step in range(2):
        out_ref[step] = prior_ref[step] + smooth_ref[place[2] * 2 + step, :, columns]


def predict_kernel(site_ref, filt_ref, out_ref):
    steps, samples, states = filt_ref.shape
    width = 128
    row = lax.broadcasted_iota(jnp.int32, (width, width), 0)
    column = lax.broadcasted_iota(jnp.int32, (width, width), 1)
    same_site = row // 4 == column // 4
    kron = jnp.zeros((width, width), f32)
    for i in range(4):
        for j in range(4):
            here = same_site & (row % 4 == i) & (column % 4 == j)
            kron = jnp.where(here, site_ref[i, j], kron)
    for k in range(0, states, width):
        rows = filt_ref[:, :, k : k + width].reshape(steps * samples, width)
        moved = lax.dot_general(
            rows, kron, ROWS_BY_ROWS, precision=highest, preferred_element_type=f32
        )
        out_ref[:, :, k : k + width] = moved.reshape(steps, samples, width)


SMEM = pl.BlockSpec(memory_space=pltpu.SMEM)
VMEM = pl.BlockSpec(memory_space=pltpu.VMEM)
HBM = pl.BlockSpec(memory_space=pltpu.HBM)


def call(kernel, name, shapes, specs, scratch=(), aliases=None):
    return pl.pallas_call(
        kernel,
        out_shape=shapes,
        in_specs=specs,
        out_specs=jax.tree.map(lambda _: VMEM, shapes),
        scratch_shapes=list(scratch),
        input_output_aliases=aliases or {},
        compiler_params=pltpu.CompilerParams(vmem_limit_bytes=VMEM_LIMIT),
        name=name,
    )


def in_hbm(value):
    return pltpu.with_memory_space_constraint(value, pltpu.HBM)


def in_vmem(value):
    return pltpu.with_memory_space_constraint(value, pltpu.VMEM)


def on_device(
    prior_path,
    observed,
    obs_mask,
    noise_draw,
    wend_blocks,
    block_cols,
    start_mean,
    trans_mats,
    gain_mats,
    smooth_mats,
    site_trans,
):
    cycle, times = lax.axis_size("blk"), lax.axis_size("tm")
    blk, samp, time = lax.axis_index("blk"), lax.axis_index("samp"), lax.axis_index("tm")
    groups = times // 2
    group, core = time // 2, time % 2
    step_count, sample_count, local_sites = noise_draw.shape
    block_sites = wend_blocks.shape[1]
    state_count = trans_mats.shape[1] * cycle
    cores = swapped(times)
    place = jnp.stack([blk, samp, core, group]).astype(jnp.int32)

    mats_shape = jax.ShapeDtypeStruct((4, cycle, trans_mats.shape[1], state_count), bf16)

    def pack(kernel, name, copies, shards, spec, held=None):
        held = () if held is None else (held,)
        made = call(
            kernel,
            name,
            mats_shape,
            [SMEM] + [spec] * len(shards) + [VMEM] * len(held),
            [pltpu.SemaphoreType.DMA((copies,))],
            {1 + len(shards): 0} if held else None,
        )(place, *shards, *held)
        return in_vmem(made)

    mats_shape = jax.ShapeDtypeStruct((4, cycle, trans_mats.shape[1], state_count), bf16)

    def pack(kernel, name, shards, held=None):
        held = () if held is None else (held,)
        made = call(
            kernel,
            name,
            mats_shape,
            [SMEM, HBM] + [VMEM] * len(held),
            [pltpu.SemaphoreType.DMA((4,))],
            {2: 0} if held else None,
        )(place, in_hbm(shards), *held)
        return in_vmem(made)

    trans_other = lax.ppermute(trans_mats, "samp", swapped(2))
    near = lax.all_gather(jnp.stack([trans_mats, trans_other]), "blk", axis=0)

    widened, mixer = noise_rim(noise_draw), noise_mixer(wend_blocks, block_cols)
    obs_noise = jnp.einsum("tsl,lm->tsm", widened, mixer, precision=highest)
    first_comp = prior_path.reshape(step_count, sample_count, local_sites, 4)[:, :, :, 0]
    seen_mask = jnp.repeat(obs_mask.astype(f32), block_sites, axis=1)
    residual = seen_mask[:, None, :] * (observed[:, None, :] - first_comp - obs_noise)
    all_resid = all_blocks(residual, "blk").transpose(1, 2, 0, 3)
    all_resid = all_resid.reshape(step_count, sample_count, local_sites * cycle)
    gain_other = lax.ppermute(gain_mats, "samp", swapped(2))
    gain = jnp.where(
        samp == 0,
        jnp.concatenate([gain_mats, gain_other], axis=2),
        jnp.concatenate([gain_other, gain_mats], axis=2),
    )
    inputs = jnp.einsum("tij,tsj->tsi", gain, all_resid, precision=highest)
    gathered = all_blocks(jnp.concatenate([inputs, start_mean[None]], axis=0), "blk")
    gathered = gathered.transpose(1, 2, 0, 3).reshape(step_count + 1, sample_count, state_count)
    near_in, start = gathered[:step_count], gathered[step_count]
    far_in = lax.ppermute(near_in, "tm", cores)
    def pack_all(near, name):
        far = lax.ppermute(near, "tm", cores)
        value = pack(functools.partial(pack_kernel, False), name, near)
        return pack(functools.partial(pack_kernel, True), name, far, value)

    near, near_in = lax.optimization_barrier((near, near_in))
    trans = pack_all(near, "pack_trans")

    smooth_mats, _ = lax.optimization_barrier((smooth_mats, all_resid))
    smooth_other = lax.ppermute(smooth_mats, "samp", swapped(2))
    near_smooth = lax.all_gather(jnp.stack([smooth_mats, smooth_other]), "blk", axis=0)

    filt_shape = jax.ShapeDtypeStruct((4, sample_count, state_count), f32)
    state_shape = jax.ShapeDtypeStruct((sample_count, state_count), f32)

    def forward(hop, state, *filtered):
        return call(
            functools.partial(forward_kernel, hop),
            "forward",
            (filt_shape, state_shape),
            [SMEM] + [VMEM] * (4 + len(filtered)),
            (),
            {5: 0} if filtered else None,
        )(place, state, near_in, far_in, trans, *filtered)

    filtered, sent = forward(0, start)
    for hop in range(1, groups):
        pairs = [(2 * hop - 2, 2 * hop), (2 * hop - 1, 2 * hop + 1)]
        state = lax.ppermute(sent, "tm", pairs)
        if hop == groups - 1:
            near_smooth, filtered = lax.optimization_barrier((near_smooth, filtered))
            smooth = pack_all(near_smooth, "pack_smooth")
            filtered, smooth = lax.optimization_barrier((filtered, smooth))
        filtered, sent = forward(hop, state, filtered)

    predicted = call(predict_kernel, "predict", filt_shape, [SMEM, VMEM])(site_trans, filtered)

    def backward(hop, state, *smoothed):
        return call(
            functools.partial(backward_kernel, hop, groups),
            "backward",
            (filt_shape, state_shape),
            [SMEM] + [VMEM] * (4 + len(smoothed)),
            (),
            {5: 0} if smoothed else None,
        )(place, state, filtered, predicted, smooth, *smoothed)

    smoothed, sent = backward(groups - 1, sent)
    for hop in range(groups - 2, -1, -1):
        pairs = [(2 * hop + 2, 2 * hop), (2 * hop + 3, 2 * hop + 1)]
        state = lax.ppermute(sent, "tm", pairs)
        smoothed, sent = backward(hop, state, smoothed)
    out_shape = jax.ShapeDtypeStruct(prior_path.shape, f32)
    return call(finish_kernel, "finish", out_shape, [SMEM, VMEM, VMEM])(place, prior_path, smoothed)


def solution(mesh):
    placed = (
        P("tm", "samp", "blk"),
        P("tm", "blk"),
        P("tm", "blk"),
        P("tm", "samp", "blk"),
        P("blk", None, None),
        P("blk"),
        P("samp", "blk"),
        P("tm", "blk", "samp"),
        P("tm", "blk", "samp"),
        P("tm", "blk", "samp"),
        P(),
    )
    return jax.shard_map(
        on_device, mesh=mesh, in_specs=placed, out_specs=P("tm", "samp", "blk"), check_vma=False
    )
```

```python
import functools
import jax
import jax.numpy as jnp
from jax import lax
from jax.experimental import pallas as pl
from jax.experimental.pallas import tpu as pltpu
from jax.sharding import PartitionSpec as P

highest = lax.Precision.HIGHEST
bf16, f32 = jnp.bfloat16, jnp.float32
ROWS_BY_ROWS = (((1,), (1,)), ((), ()))
VMEM_LIMIT = 2 * 1024 * 1024


def ring(count, step):
    return [(i, (i + step) % count) for i in range(count)]


def swapped(count):
    return [(i, i ^ 1) for i in range(count)]


def all_blocks(value, axis):
    count = lax.axis_size(axis)
    copies = jnp.broadcast_to(value[None], (count,) + value.shape)
    return lax.all_to_all(copies, axis, 0, 0, tiled=True)


def noise_rim(noise_draw, rim=16):
    cycle, local_sites = lax.axis_size("blk"), noise_draw.shape[2]
    before = lax.ppermute(noise_draw[:, :, local_sites - rim :], "blk", ring(cycle, 1))
    after = lax.ppermute(noise_draw[:, :, :rim], "blk", ring(cycle, -1))
    return jnp.concatenate([before, noise_draw, after], axis=2)


def noise_mixer(wend_blocks, block_cols):
    block_sites = wend_blocks.shape[1]
    local_blocks = block_cols.shape[0] // 4
    cycle = lax.axis_size("blk")
    pair_rows = jnp.arange(local_blocks * 4, dtype=jnp.int32) // 4
    first_block = lax.axis_index("blk") * local_blocks
    offset = (block_cols - first_block - pair_rows + 2) % (local_blocks * cycle)
    chooser = (
        (pair_rows + offset)[:, None] == jnp.arange(local_blocks + 4, dtype=jnp.int32)[None, :]
    ).astype(f32)
    blocks = wend_blocks.reshape(local_blocks, 4, block_sites, block_sites)
    chooser = chooser.reshape(local_blocks, 4, local_blocks + 4)
    mixer = jnp.sum(chooser[:, :, :, None, None] * blocks[:, :, None, :, :], axis=1)
    return mixer.transpose(1, 3, 0, 2).reshape(
        (local_blocks + 4) * block_sites, local_blocks * block_sites
    )


def split_rows(value):
    high = value.astype(bf16)
    low = (value - high.astype(f32)).astype(bf16)
    return jnp.concatenate([high, low], axis=0)


def joined_rows(value):
    rows = value.shape[0] // 2
    return value[:rows] + value[rows:]


def pack_kernel(parts, rows_ref, out_ref, sems):
    cores, count, steps = rows_ref.shape[:3]
    copies = []
    for core in range(cores):
        for step in range(steps):
            for part in range(parts):
                blocks = pl.ds(part * (count // parts), count // parts)
                copy = pltpu.make_async_copy(
                    rows_ref.at[core, blocks, step],
                    out_ref.at[core * steps + step, blocks],
                    sems.at[len(copies)],
                )
                copy.start()
                copies.append(copy)
    for copy in copies:
        copy.wait()


def apply_rows(mats, turn, value, store):
    count, rows, _ = mats.shape[1:]
    terms = split_rows(value)
    for k in range(0, count, 2):
        block = jnp.concatenate([mats[turn, k], mats[turn, k + 1]], axis=0)
        part = lax.dot_general(terms, block, ROWS_BY_ROWS, preferred_element_type=f32)
        store(slice(k * rows, (k + 2) * rows), joined_rows(part))


def forward_kernel(hop, state_ref, near_in, far_in, mats, *refs):
    filt_ref, sent_ref = refs[-2:]

    @pl.when(lax.axis_index("chip") == hop)
    def _():
        sent_ref[...] = state_ref[...]

        def step(turn, carry):
            is_near = turn // 2 == lax.axis_index("core")

            def store(columns, part):
                at = lax.rem(turn, 2)
                added = jnp.where(is_near, near_in[at, :, columns], far_in[at, :, columns])
                filt_ref[turn, :, columns] = part + added

            apply_rows(mats, turn, sent_ref[...], store)
            sent_ref[...] = filt_ref[turn]
            return carry

        lax.fori_loop(0, 4, step, 0)


def backward_kernel(hop, hops, state_ref, filt_ref, pred_ref, mats, *refs):
    target_ref, sent_ref = refs[-2:]

    @pl.when(lax.axis_index("chip") == hop)
    def _():
        sent_ref[...] = state_ref[...]

        def step(i, carry):
            turn = 3 - i
            change = sent_ref[...] - pred_ref[turn]
            if hop == hops - 1:
                change = jnp.where(turn == 3, 0.0, change)

            def store(columns, part):
                target_ref[turn, :, columns] = filt_ref[turn, :, columns] + part

            apply_rows(mats, turn, change, store)
            sent_ref[...] = target_ref[turn]
            return carry

        lax.fori_loop(0, 4, step, 0)


def finish_kernel(prior_ref, smooth_ref, out_ref):
    width = out_ref.shape[2]
    columns = pl.ds(pl.multiple_of(lax.axis_index("blk") * width, 128), width)
    for step in range(2):
        out_ref[step] = prior_ref[step] + smooth_ref[lax.axis_index("core") * 2 + step, :, columns]


def kron_kernel(site_ref, out_ref):
    row = lax.broadcasted_iota(jnp.int32, out_ref.shape, 0)
    column = lax.broadcasted_iota(jnp.int32, out_ref.shape, 1)
    same_site = row // 4 == column // 4
    kron = jnp.zeros(out_ref.shape, f32)
    for i in range(4):
        for j in range(4):
            here = same_site & (row % 4 == i) & (column % 4 == j)
            kron = jnp.where(here, site_ref[i, j], kron)
    out_ref[...] = kron


def predict_kernel(kron_ref, filt_ref, out_ref):
    steps, samples, states = filt_ref.shape
    width = kron_ref.shape[0]
    for k in range(0, states, width):
        rows = filt_ref[:, :, k : k + width].reshape(steps * samples, width)
        moved = lax.dot_general(
            rows, kron_ref[...], ROWS_BY_ROWS, precision=highest, preferred_element_type=f32
        )
        out_ref[:, :, k : k + width] = moved.reshape(steps, samples, width)


SMEM = pl.BlockSpec(memory_space=pltpu.SMEM)
VMEM = pl.BlockSpec(memory_space=pltpu.VMEM)
HBM = pl.BlockSpec(memory_space=pltpu.HBM)


def call(kernel, name, shapes, specs, scratch=(), aliases=None):
    return pl.pallas_call(
        kernel,
        out_shape=shapes,
        in_specs=specs,
        out_specs=jax.tree.map(lambda _: VMEM, shapes),
        scratch_shapes=list(scratch),
        input_output_aliases=aliases or {},
        compiler_params=pltpu.CompilerParams(vmem_limit_bytes=VMEM_LIMIT),
        name=name,
    )


def in_hbm(value):
    return pltpu.with_memory_space_constraint(value, pltpu.HBM)


def in_vmem(value):
    return pltpu.with_memory_space_constraint(value, pltpu.VMEM)


def on_device(
    prior_path,
    observed,
    obs_mask,
    noise_draw,
    wend_blocks,
    block_cols,
    start_mean,
    trans_mats,
    gain_mats,
    smooth_mats,
    site_trans,
):
    cycle, groups = lax.axis_size("blk"), lax.axis_size("chip")
    step_count, sample_count, local_sites = noise_draw.shape
    block_sites = wend_blocks.shape[1]
    state_count = trans_mats.shape[1] * cycle

    mats_shape = jax.ShapeDtypeStruct((4, cycle, trans_mats.shape[1], state_count), bf16)

    def all_rows(mats):
        whole = lax.all_gather(mats, "samp", axis=2, tiled=True)
        rows = lax.all_gather(whole, ("core", "blk"), axis=0)
        return rows.reshape((2, cycle) + rows.shape[1:])

    def pack(rows, name):
        parts = 4
        made = call(
            functools.partial(pack_kernel, parts),
            name,
            mats_shape,
            [HBM],
            [pltpu.SemaphoreType.DMA((4 * parts,))],
        )(in_hbm(rows))
        return in_vmem(made)

    trans_rows = all_rows(trans_mats)

    widened, mixer = noise_rim(noise_draw), noise_mixer(wend_blocks, block_cols)
    obs_noise = jnp.einsum("tsl,lm->tsm", widened, mixer, precision=highest)
    first_comp = prior_path.reshape(step_count, sample_count, local_sites, 4)[:, :, :, 0]
    seen_mask = jnp.repeat(obs_mask.astype(f32), block_sites, axis=1)
    residual = seen_mask[:, None, :] * (observed[:, None, :] - first_comp - obs_noise)
    all_resid = all_blocks(residual, "blk").transpose(1, 2, 0, 3)
    all_resid = all_resid.reshape(step_count, sample_count, local_sites * cycle)
    gain = lax.all_gather(gain_mats, "samp", axis=2, tiled=True)
    inputs = jnp.einsum("tij,tsj->tsi", gain, all_resid, precision=highest)
    gathered = all_blocks(jnp.concatenate([inputs, start_mean[None]], axis=0), "blk")
    gathered = gathered.transpose(1, 2, 0, 3).reshape(step_count + 1, sample_count, state_count)
    near_in, start = gathered[:step_count], gathered[step_count]
    far_in = lax.ppermute(near_in, "core", swapped(2))
    trans_rows, near_in = lax.optimization_barrier((trans_rows, near_in))
    trans = pack(trans_rows, "pack_trans")

    smooth_mats, _ = lax.optimization_barrier((smooth_mats, all_resid))
    smooth_rows = all_rows(smooth_mats)

    filt_shape = jax.ShapeDtypeStruct((4, sample_count, state_count), f32)
    state_shape = jax.ShapeDtypeStruct((sample_count, state_count), f32)

    def forward(hop, state, *filtered):
        return call(
            functools.partial(forward_kernel, hop),
            "forward",
            (filt_shape, state_shape),
            [VMEM] * (4 + len(filtered)),
            (),
            {4: 0} if filtered else None,
        )(state, near_in, far_in, trans, *filtered)

    kron_shape = jax.ShapeDtypeStruct((128, 128), f32)
    kron = in_vmem(call(kron_kernel, "kron", kron_shape, [SMEM])(site_trans))
    kron, start = lax.optimization_barrier((kron, start))
    filtered, sent = forward(0, start)
    for hop in range(1, groups):
        state = lax.ppermute(sent, "chip", [(hop - 1, hop)])
        if hop == groups - 1:
            smooth_rows, filtered = lax.optimization_barrier((smooth_rows, filtered))
            smooth = pack(smooth_rows, "pack_smooth")
            filtered, smooth = lax.optimization_barrier((filtered, smooth))
        filtered, sent = forward(hop, state, filtered)

    predicted = call(predict_kernel, "predict", filt_shape, [VMEM, VMEM])(kron, filtered)

    def backward(hop, state, *smoothed):
        return call(
            functools.partial(backward_kernel, hop, groups),
            "backward",
            (filt_shape, state_shape),
            [VMEM] * (4 + len(smoothed)),
            (),
            {4: 0} if smoothed else None,
        )(state, filtered, predicted, smooth, *smoothed)

    smoothed, sent = backward(groups - 1, sent)
    for hop in range(groups - 2, -1, -1):
        state = lax.ppermute(sent, "chip", [(hop + 1, hop)])
        smoothed, sent = backward(hop, state, smoothed)
    out_shape = jax.ShapeDtypeStruct(prior_path.shape, f32)
    return call(finish_kernel, "finish", out_shape, [VMEM, VMEM])(prior_path, smoothed)


def solution(mesh):
    times, cycle, samples = mesh.devices.shape
    by_chip = jax.sharding.Mesh(
        mesh.devices.reshape(times // 2, 2, cycle, samples), ("chip", "core", "blk", "samp")
    )
    time = ("chip", "core")
    placed = (
        P(time, "samp", "blk"),
        P(time, "blk"),
        P(time, "blk"),
        P(time, "samp", "blk"),
        P("blk", None, None),
        P("blk"),
        P("samp", "blk"),
        P(time, "blk", "samp"),
        P(time, "blk", "samp"),
        P(time, "blk", "samp"),
        P(),
    )
    return jax.shard_map(
        on_device, mesh=by_chip, in_specs=placed, out_specs=P(time, "samp", "blk"), check_vma=False
    )
```

```python
import functools
import jax
import jax.numpy as jnp
from jax import lax
from jax.experimental import pallas as pl
from jax.experimental.pallas import tpu as pltpu
from jax.sharding import PartitionSpec as P

highest = lax.Precision.HIGHEST
bf16, f32 = jnp.bfloat16, jnp.float32
ROWS_BY_ROWS = (((1,), (1,)), ((), ()))
VMEM_LIMIT = 2 * 1024 * 1024


def ring(count, step):
    return [(i, (i + step) % count) for i in range(count)]


def swapped(count):
    return [(i, i ^ 1) for i in range(count)]


def all_blocks(value, axis):
    count = lax.axis_size(axis)
    copies = jnp.broadcast_to(value[None], (count,) + value.shape)
    return lax.all_to_all(copies, axis, 0, 0, tiled=True)


def noise_rim(noise_draw, rim=16):
    cycle, local_sites = lax.axis_size("blk"), noise_draw.shape[2]
    before = lax.ppermute(noise_draw[:, :, local_sites - rim :], "blk", ring(cycle, 1))
    after = lax.ppermute(noise_draw[:, :, :rim], "blk", ring(cycle, -1))
    return jnp.concatenate([before, noise_draw, after], axis=2)


def noise_mixer(wend_blocks, block_cols):
    block_sites = wend_blocks.shape[1]
    local_blocks = block_cols.shape[0] // 4
    cycle = lax.axis_size("blk")
    pair_rows = jnp.arange(local_blocks * 4, dtype=jnp.int32) // 4
    first_block = lax.axis_index("blk") * local_blocks
    offset = (block_cols - first_block - pair_rows + 2) % (local_blocks * cycle)
    chooser = (
        (pair_rows + offset)[:, None] == jnp.arange(local_blocks + 4, dtype=jnp.int32)[None, :]
    ).astype(f32)
    blocks = wend_blocks.reshape(local_blocks, 4, block_sites, block_sites)
    chooser = chooser.reshape(local_blocks, 4, local_blocks + 4)
    mixer = jnp.sum(chooser[:, :, :, None, None] * blocks[:, :, None, :, :], axis=1)
    return mixer.transpose(1, 3, 0, 2).reshape(
        (local_blocks + 4) * block_sites, local_blocks * block_sites
    )


def split_rows(value):
    high = value.astype(bf16)
    low = (value - high.astype(f32)).astype(bf16)
    return jnp.concatenate([high, low], axis=0)


def joined_rows(value):
    rows = value.shape[0] // 2
    return value[:rows] + value[rows:]


def start_pack(rows_ref, mats_ref, sems, order):
    steps, started = rows_ref.shape[2], {}
    for turn in order:
        started[turn] = []
        for part in range(sems.shape[1]):
            size = rows_ref.shape[1] // sems.shape[1]
            blocks = pl.ds(part * size, size)
            copy = pltpu.make_async_copy(
                rows_ref.at[turn // steps, blocks, turn % steps],
                mats_ref.at[turn, blocks],
                sems.at[turn, part],
            )
            copy.start()
            started[turn].append(copy)
    return started


def apply_rows(mats, turn, value, store):
    count, rows, _ = mats.shape[1:]
    terms = split_rows(value)
    for k in range(0, count, 2):
        block = jnp.concatenate([mats[turn, k], mats[turn, k + 1]], axis=0)
        part = lax.dot_general(terms, block, ROWS_BY_ROWS, preferred_element_type=f32)
        store(slice(k * rows, (k + 2) * rows), joined_rows(part))


def apply_columns(flipped, turn, value, store):
    terms = split_rows(value)
    for k in range(0, flipped.shape[2], 512):
        columns = slice(k, k + 512)
        part = jnp.dot(terms, flipped[turn, :, columns], preferred_element_type=f32)
        store(columns, joined_rows(part))


def flip_kernel(mats_ref, out_ref):
    rows = mats_ref.shape[2]

    def step(turn, carry):
        for k in range(0, mats_ref.shape[1], 2):
            block = jnp.concatenate([mats_ref[turn, k], mats_ref[turn, k + 1]], axis=0)
            for j in range(0, block.shape[1], 256):
                out_ref[turn, j : j + 256, k * rows : (k + 2) * rows] = block[:, j : j + 256].T
        return carry

    lax.fori_loop(0, mats_ref.shape[0], step, 0)


def forward_step(apply, mats, turn, near_in, far_in, filt_ref, sent_ref):
    is_near = turn // 2 == lax.axis_index("core")

    def store(columns, part):
        at = lax.rem(turn, 2)
        added = jnp.where(is_near, near_in[at, :, columns], far_in[at, :, columns])
        filt_ref[turn, :, columns] = part + added

    apply(mats, turn, sent_ref[...], store)
    sent_ref[...] = filt_ref[turn]


def forward_first_kernel(state_ref, near_in, far_in, rows_ref, mats_ref, filt_ref, sent_ref, sems):
    copies = start_pack(rows_ref, mats_ref, sems, range(4))
    sent_ref[...] = state_ref[...]
    for turn in range(4):
        for copy in copies[turn]:
            copy.wait()

        @pl.when(lax.axis_index("chip") == 0)
        def _():
            at = jnp.int32(turn)
            forward_step(apply_rows, mats_ref, at, near_in, far_in, filt_ref, sent_ref)


def forward_kernel(hop, state_ref, near_in, far_in, mats, held_ref, filt_ref, sent_ref):
    @pl.when(lax.axis_index("chip") == hop)
    def _():
        sent_ref[...] = state_ref[...]

        def step(turn, carry):
            forward_step(apply_columns, mats, turn, near_in, far_in, filt_ref, sent_ref)
            return carry

        lax.fori_loop(0, 4, step, 0)


def backward_step(apply, mats, turn, filt_ref, pred_ref, out_ref, sent_ref):
    def store(columns, part):
        out_ref[turn, :, columns] = filt_ref[turn, :, columns] + part

    apply(mats, turn, sent_ref[...] - pred_ref[turn], store)
    sent_ref[...] = out_ref[turn]


def backward_first_kernel(filt_ref, pred_ref, rows_ref, mats_ref, out_ref, sent_ref, sems):
    copies = start_pack(rows_ref, mats_ref, sems, (2, 1, 0, 3))
    out_ref[3] = filt_ref[3]
    sent_ref[...] = filt_ref[3]
    for turn in (2, 1, 0):
        for copy in copies[turn]:
            copy.wait()

        @pl.when(lax.axis_index("chip") == lax.axis_size("chip") - 1)
        def _():
            at = jnp.int32(turn)
            backward_step(apply_rows, mats_ref, at, filt_ref, pred_ref, out_ref, sent_ref)

    for copy in copies[3]:
        copy.wait()


def backward_kernel(hop, state_ref, filt_ref, pred_ref, mats, held_ref, out_ref, sent_ref):
    @pl.when(lax.axis_index("chip") == hop)
    def _():
        sent_ref[...] = state_ref[...]

        def step(i, carry):
            backward_step(apply_columns, mats, 3 - i, filt_ref, pred_ref, out_ref, sent_ref)
            return carry

        lax.fori_loop(0, 4, step, 0)


def finish_kernel(prior_ref, smooth_ref, out_ref):
    width = out_ref.shape[2]
    columns = pl.ds(pl.multiple_of(lax.axis_index("blk") * width, 128), width)
    for step in range(2):
        out_ref[step] = prior_ref[step] + smooth_ref[lax.axis_index("core") * 2 + step, :, columns]


def kron_kernel(site_ref, out_ref):
    row = lax.broadcasted_iota(jnp.int32, out_ref.shape, 0)
    column = lax.broadcasted_iota(jnp.int32, out_ref.shape, 1)
    same_site = row // 4 == column // 4
    kron = jnp.zeros(out_ref.shape, f32)
    for i in range(4):
        for j in range(4):
            here = same_site & (row % 4 == i) & (column % 4 == j)
            kron = jnp.where(here, site_ref[i, j], kron)
    out_ref[...] = kron


def predict_kernel(kron_ref, filt_ref, out_ref):
    steps, samples, states = filt_ref.shape
    width = kron_ref.shape[0]
    for k in range(0, states, width):
        rows = filt_ref[:, :, k : k + width].reshape(steps * samples, width)
        moved = lax.dot_general(
            rows, kron_ref[...], ROWS_BY_ROWS, precision=highest, preferred_element_type=f32
        )
        out_ref[:, :, k : k + width] = moved.reshape(steps, samples, width)


SMEM = pl.BlockSpec(memory_space=pltpu.SMEM)
VMEM = pl.BlockSpec(memory_space=pltpu.VMEM)
HBM = pl.BlockSpec(memory_space=pltpu.HBM)


def call(kernel, name, shapes, specs, scratch=(), aliases=None):
    return pl.pallas_call(
        kernel,
        out_shape=shapes,
        in_specs=specs,
        out_specs=jax.tree.map(lambda _: VMEM, shapes),
        scratch_shapes=list(scratch),
        input_output_aliases=aliases or {},
        compiler_params=pltpu.CompilerParams(vmem_limit_bytes=VMEM_LIMIT),
        name=name,
    )


def in_hbm(value):
    return pltpu.with_memory_space_constraint(value, pltpu.HBM)


def in_vmem(value):
    return pltpu.with_memory_space_constraint(value, pltpu.VMEM)


def on_device(
    prior_path,
    observed,
    obs_mask,
    noise_draw,
    wend_blocks,
    block_cols,
    start_mean,
    trans_mats,
    gain_mats,
    smooth_mats,
    site_trans,
):
    cycle, groups = lax.axis_size("blk"), lax.axis_size("chip")
    step_count, sample_count, local_sites = noise_draw.shape
    block_sites = wend_blocks.shape[1]
    state_count = trans_mats.shape[1] * cycle

    mats_shape = jax.ShapeDtypeStruct((4, cycle, trans_mats.shape[1], state_count), bf16)

    def all_rows(mats):
        whole = lax.all_gather(mats, "samp", axis=2, tiled=True)
        rows = lax.all_gather(whole, ("core", "blk"), axis=0)
        return rows.reshape((2, cycle) + rows.shape[1:])

    def flip(mats, name):
        shape = jax.ShapeDtypeStruct((4, state_count, state_count), bf16)
        return in_vmem(call(flip_kernel, name, shape, [VMEM])(mats))

    trans_rows = all_rows(trans_mats)

    widened, mixer = noise_rim(noise_draw), noise_mixer(wend_blocks, block_cols)
    obs_noise = jnp.einsum("tsl,lm->tsm", widened, mixer, precision=highest)
    first_comp = prior_path.reshape(step_count, sample_count, local_sites, 4)[:, :, :, 0]
    seen_mask = jnp.repeat(obs_mask.astype(f32), block_sites, axis=1)
    residual = seen_mask[:, None, :] * (observed[:, None, :] - first_comp - obs_noise)
    all_resid = all_blocks(residual, "blk").transpose(1, 2, 0, 3)
    all_resid = all_resid.reshape(step_count, sample_count, local_sites * cycle)
    gain = lax.all_gather(gain_mats, "samp", axis=2, tiled=True)
    inputs = jnp.einsum("tij,tsj->tsi", gain, all_resid, precision=highest)
    gathered = all_blocks(jnp.concatenate([inputs, start_mean[None]], axis=0), "blk")
    gathered = gathered.transpose(1, 2, 0, 3).reshape(step_count + 1, sample_count, state_count)
    near_in, start = gathered[:step_count], gathered[step_count]
    far_in = lax.ppermute(near_in, "core", swapped(2))
    trans_rows, near_in = lax.optimization_barrier((trans_rows, near_in))

    smooth_mats, _ = lax.optimization_barrier((smooth_mats, all_resid))
    smooth_rows = all_rows(smooth_mats)

    filt_shape = jax.ShapeDtypeStruct((4, sample_count, state_count), f32)
    state_shape = jax.ShapeDtypeStruct((sample_count, state_count), f32)

    kron_shape = jax.ShapeDtypeStruct((128, 128), f32)
    kron = in_vmem(call(kron_kernel, "kron", kron_shape, [SMEM])(site_trans))
    kron, start = lax.optimization_barrier((kron, start))
    dmas = [pltpu.SemaphoreType.DMA((4, 4))]
    shapes = (mats_shape, filt_shape, state_shape)
    trans, filtered, sent = call(
        forward_first_kernel, "forward_first", shapes, [VMEM] * 3 + [HBM], dmas
    )(start, near_in, far_in, in_hbm(trans_rows))
    trans = flip(in_vmem(trans), "flip_trans")
    for hop in range(1, groups):
        state = lax.ppermute(sent, "chip", [(hop - 1, hop)])
        kernel = functools.partial(forward_kernel, hop)
        filtered, sent = call(kernel, "forward", shapes[1:], [VMEM] * 5, (), {4: 0})(
            state, near_in, far_in, trans, filtered
        )

    predicted = call(predict_kernel, "predict", filt_shape, [VMEM, VMEM])(kron, filtered)
    smooth_rows, predicted = lax.optimization_barrier((smooth_rows, predicted))
    smooth, smoothed, sent = call(
        backward_first_kernel, "backward_first", shapes, [VMEM] * 2 + [HBM], dmas
    )(filtered, predicted, in_hbm(smooth_rows))
    smooth = flip(in_vmem(smooth), "flip_smooth")
    for hop in range(groups - 2, -1, -1):
        state = lax.ppermute(sent, "chip", [(hop + 1, hop)])
        kernel = functools.partial(backward_kernel, hop)
        smoothed, sent = call(kernel, "backward", shapes[1:], [VMEM] * 5, (), {4: 0})(
            state, filtered, predicted, smooth, smoothed
        )
    out_shape = jax.ShapeDtypeStruct(prior_path.shape, f32)
    return call(finish_kernel, "finish", out_shape, [VMEM, VMEM])(prior_path, smoothed)


def solution(mesh):
    times, cycle, samples = mesh.devices.shape
    by_chip = jax.sharding.Mesh(
        mesh.devices.reshape(times // 2, 2, cycle, samples), ("chip", "core", "blk", "samp")
    )
    time = ("chip", "core")
    placed = (
        P(time, "samp", "blk"),
        P(time, "blk"),
        P(time, "blk"),
        P(time, "samp", "blk"),
        P("blk", None, None),
        P("blk"),
        P("samp", "blk"),
        P(time, "blk", "samp"),
        P(time, "blk", "samp"),
        P(time, "blk", "samp"),
        P(),
    )
    return jax.shard_map(
        on_device, mesh=by_chip, in_specs=placed, out_specs=P(time, "samp", "blk"), check_vma=False
    )
```

```python
import functools
import jax
import jax.numpy as jnp
from jax import lax
from jax.experimental import pallas as pl
from jax.experimental.pallas import tpu as pltpu
from jax.sharding import PartitionSpec as P

highest = lax.Precision.HIGHEST
bf16, f32 = jnp.bfloat16, jnp.float32
ROWS_BY_ROWS = (((1,), (1,)), ((), ()))
VMEM_LIMIT = 2 * 1024 * 1024
CHUNK = 256


def ring(count, step):
    return [(i, (i + step) % count) for i in range(count)]


def swapped(count):
    return [(i, i ^ 1) for i in range(count)]


def all_blocks(value, axis):
    count = lax.axis_size(axis)
    copies = jnp.broadcast_to(value[None], (count,) + value.shape)
    return lax.all_to_all(copies, axis, 0, 0, tiled=True)


def noise_rim(noise_draw, rim=16):
    cycle, local_sites = lax.axis_size("blk"), noise_draw.shape[2]
    before = lax.ppermute(noise_draw[:, :, local_sites - rim :], "blk", ring(cycle, 1))
    after = lax.ppermute(noise_draw[:, :, :rim], "blk", ring(cycle, -1))
    return jnp.concatenate([before, noise_draw, after], axis=2)


def noise_mixer(wend_blocks, block_cols):
    block_sites = wend_blocks.shape[1]
    local_blocks = block_cols.shape[0] // 4
    cycle = lax.axis_size("blk")
    pair_rows = jnp.arange(local_blocks * 4, dtype=jnp.int32) // 4
    first_block = lax.axis_index("blk") * local_blocks
    offset = (block_cols - first_block - pair_rows + 2) % (local_blocks * cycle)
    chooser = (
        (pair_rows + offset)[:, None] == jnp.arange(local_blocks + 4, dtype=jnp.int32)[None, :]
    ).astype(f32)
    blocks = wend_blocks.reshape(local_blocks, 4, block_sites, block_sites)
    chooser = chooser.reshape(local_blocks, 4, local_blocks + 4)
    mixer = jnp.sum(chooser[:, :, :, None, None] * blocks[:, :, None, :, :], axis=1)
    return mixer.transpose(1, 3, 0, 2).reshape(
        (local_blocks + 4) * block_sites, local_blocks * block_sites
    )


def split_rows(value):
    high = value.astype(bf16)
    low = (value - high.astype(f32)).astype(bf16)
    return jnp.concatenate([high, low], axis=0)


def joined_rows(value):
    rows = value.shape[0] // 2
    return value[:rows] + value[rows:]


def start_pack(rows_ref, mats_ref, sems, order):
    steps, started = rows_ref.shape[2], {}
    for turn in order:
        started[turn] = []
        for part in range(sems.shape[1]):
            size = rows_ref.shape[1] // sems.shape[1]
            blocks = pl.ds(part * size, size)
            copy = pltpu.make_async_copy(
                rows_ref.at[turn // steps, blocks, turn % steps],
                mats_ref.at[turn, blocks],
                sems.at[turn, part],
            )
            copy.start()
            started[turn].append(copy)
    return started


def apply_rows(mats, turn, value, store):
    count, rows, _ = mats.shape[1:]
    terms = split_rows(value)
    for k in range(0, count, 2):
        block = jnp.concatenate([mats[turn, k], mats[turn, k + 1]], axis=0)
        part = lax.dot_general(terms, block, ROWS_BY_ROWS, preferred_element_type=f32)
        store(slice(k * rows, (k + 2) * rows), joined_rows(part))


def in_chunks(ref):
    return [slice(k, k + CHUNK) for k in range(0, ref.shape[-1], CHUNK)]


def apply_columns(flipped, turn, values):
    terms = [split_rows(value) for value in values]
    chunks = in_chunks(flipped)
    return [
        joined_rows(
            sum(
                jnp.dot(term, flipped[turn, rows, columns], preferred_element_type=f32)
                for term, rows in zip(terms, chunks)
            )
        )
        for columns in chunks
    ]


def flip_kernel(mats_ref, out_ref):
    rows = mats_ref.shape[2]

    def step(turn, carry):
        for k in range(0, mats_ref.shape[1], 2):
            block = jnp.concatenate([mats_ref[turn, k], mats_ref[turn, k + 1]], axis=0)
            for j in range(0, block.shape[1], 256):
                out_ref[turn, j : j + 256, k * rows : (k + 2) * rows] = block[:, j : j + 256].T
        return carry

    lax.fori_loop(0, mats_ref.shape[0], step, 0)


def forward_step(apply, mats, turn, near_in, far_in, filt_ref, sent_ref):
    is_near = turn // 2 == lax.axis_index("core")

    def store(columns, part):
        at = lax.rem(turn, 2)
        added = jnp.where(is_near, near_in[at, :, columns], far_in[at, :, columns])
        filt_ref[turn, :, columns] = part + added

    apply(mats, turn, sent_ref[...], store)
    sent_ref[...] = filt_ref[turn]


def forward_first_kernel(state_ref, near_in, far_in, rows_ref, mats_ref, filt_ref, sent_ref, sems):
    copies = start_pack(rows_ref, mats_ref, sems, range(4))
    sent_ref[...] = state_ref[...]
    for turn in range(4):
        for copy in copies[turn]:
            copy.wait()

        @pl.when(lax.axis_index("chip") == 0)
        def _():
            at = jnp.int32(turn)
            forward_step(apply_rows, mats_ref, at, near_in, far_in, filt_ref, sent_ref)


def forward_kernel(hop, state_ref, near_in, far_in, mats, held_ref, filt_ref, sent_ref):
    @pl.when(lax.axis_index("chip") == hop)
    def _():
        chunks = in_chunks(state_ref)
        state = [state_ref[:, columns] for columns in chunks]
        first = lax.axis_index("core") == 0
        for turn in range(4):
            parts = apply_columns(mats, turn, state)
            for n, columns in enumerate(chunks):
                inputs = (near_in[turn % 2, :, columns], far_in[turn % 2, :, columns])
                state[n] = parts[n] + jnp.where(first, *(inputs if turn < 2 else inputs[::-1]))
                filt_ref[turn, :, columns] = state[n]
                if turn == 3:
                    sent_ref[:, columns] = state[n]


def backward_step(apply, mats, turn, filt_ref, pred_ref, out_ref, sent_ref):
    def store(columns, part):
        out_ref[turn, :, columns] = filt_ref[turn, :, columns] + part

    apply(mats, turn, sent_ref[...] - pred_ref[turn], store)
    sent_ref[...] = out_ref[turn]


def backward_first_kernel(filt_ref, pred_ref, rows_ref, mats_ref, out_ref, sent_ref, sems):
    copies = start_pack(rows_ref, mats_ref, sems, (2, 1, 0, 3))
    out_ref[3] = filt_ref[3]
    sent_ref[...] = filt_ref[3]
    for turn in (2, 1, 0):
        for copy in copies[turn]:
            copy.wait()

        @pl.when(lax.axis_index("chip") == lax.axis_size("chip") - 1)
        def _():
            at = jnp.int32(turn)
            backward_step(apply_rows, mats_ref, at, filt_ref, pred_ref, out_ref, sent_ref)

    for copy in copies[3]:
        copy.wait()


def backward_kernel(hop, state_ref, filt_ref, pred_ref, mats, held_ref, out_ref, sent_ref):
    @pl.when(lax.axis_index("chip") == hop)
    def _():
        chunks = in_chunks(state_ref)
        state = [state_ref[:, columns] for columns in chunks]
        for turn in range(3, -1, -1):
            change = [state[n] - pred_ref[turn, :, columns] for n, columns in enumerate(chunks)]
            parts = apply_columns(mats, turn, change)
            for n, columns in enumerate(chunks):
                state[n] = filt_ref[turn, :, columns] + parts[n]
                out_ref[turn, :, columns] = state[n]
                if turn == 0:
                    sent_ref[:, columns] = state[n]


def finish_kernel(prior_ref, smooth_ref, out_ref):
    width = out_ref.shape[2]
    columns = pl.ds(pl.multiple_of(lax.axis_index("blk") * width, 128), width)
    for step in range(2):
        out_ref[step] = prior_ref[step] + smooth_ref[lax.axis_index("core") * 2 + step, :, columns]


def kron_kernel(site_ref, out_ref):
    row = lax.broadcasted_iota(jnp.int32, out_ref.shape, 0)
    column = lax.broadcasted_iota(jnp.int32, out_ref.shape, 1)
    same_site = row // 4 == column // 4
    kron = jnp.zeros(out_ref.shape, f32)
    for i in range(4):
        for j in range(4):
            here = same_site & (row % 4 == i) & (column % 4 == j)
            kron = jnp.where(here, site_ref[i, j], kron)
    out_ref[...] = kron


def predict_kernel(kron_ref, filt_ref, out_ref):
    steps, samples, states = filt_ref.shape
    width = kron_ref.shape[0]
    for k in range(0, states, width):
        rows = filt_ref[:, :, k : k + width].reshape(steps * samples, width)
        moved = lax.dot_general(
            rows, kron_ref[...], ROWS_BY_ROWS, precision=highest, preferred_element_type=f32
        )
        out_ref[:, :, k : k + width] = moved.reshape(steps, samples, width)


SMEM = pl.BlockSpec(memory_space=pltpu.SMEM)
VMEM = pl.BlockSpec(memory_space=pltpu.VMEM)
HBM = pl.BlockSpec(memory_space=pltpu.HBM)


def call(kernel, name, shapes, specs, scratch=(), aliases=None):
    return pl.pallas_call(
        kernel,
        out_shape=shapes,
        in_specs=specs,
        out_specs=jax.tree.map(lambda _: VMEM, shapes),
        scratch_shapes=list(scratch),
        input_output_aliases=aliases or {},
        compiler_params=pltpu.CompilerParams(vmem_limit_bytes=VMEM_LIMIT),
        name=name,
    )


def in_hbm(value):
    return pltpu.with_memory_space_constraint(value, pltpu.HBM)


def in_vmem(value):
    return pltpu.with_memory_space_constraint(value, pltpu.VMEM)


def on_device(
    prior_path,
    observed,
    obs_mask,
    noise_draw,
    wend_blocks,
    block_cols,
    start_mean,
    trans_mats,
    gain_mats,
    smooth_mats,
    site_trans,
):
    cycle, groups = lax.axis_size("blk"), lax.axis_size("chip")
    step_count, sample_count, local_sites = noise_draw.shape
    block_sites = wend_blocks.shape[1]
    state_count = trans_mats.shape[1] * cycle

    mats_shape = jax.ShapeDtypeStruct((4, cycle, trans_mats.shape[1], state_count), bf16)

    def all_rows(mats):
        whole = lax.all_gather(mats, "samp", axis=2, tiled=True)
        rows = lax.all_gather(whole, ("core", "blk"), axis=0)
        return rows.reshape((2, cycle) + rows.shape[1:])

    def flip(mats, name):
        shape = jax.ShapeDtypeStruct((4, state_count, state_count), bf16)
        return in_vmem(call(flip_kernel, name, shape, [VMEM])(mats))

    trans_rows = all_rows(trans_mats)

    widened, mixer = noise_rim(noise_draw), noise_mixer(wend_blocks, block_cols)
    obs_noise = jnp.einsum("tsl,lm->tsm", widened, mixer, precision=highest)
    first_comp = prior_path.reshape(step_count, sample_count, local_sites, 4)[:, :, :, 0]
    seen_mask = jnp.repeat(obs_mask.astype(f32), block_sites, axis=1)
    residual = seen_mask[:, None, :] * (observed[:, None, :] - first_comp - obs_noise)
    all_resid = all_blocks(residual, "blk").transpose(1, 2, 0, 3)
    all_resid = all_resid.reshape(step_count, sample_count, local_sites * cycle)
    gain = lax.all_gather(gain_mats, "samp", axis=2, tiled=True)
    inputs = jnp.einsum("tij,tsj->tsi", gain, all_resid, precision=highest)
    gathered = all_blocks(jnp.concatenate([inputs, start_mean[None]], axis=0), "blk")
    gathered = gathered.transpose(1, 2, 0, 3).reshape(step_count + 1, sample_count, state_count)
    near_in, start = gathered[:step_count], gathered[step_count]
    far_in = lax.ppermute(near_in, "core", swapped(2))
    trans_rows, near_in = lax.optimization_barrier((trans_rows, near_in))

    smooth_mats, _ = lax.optimization_barrier((smooth_mats, all_resid))
    smooth_rows = all_rows(smooth_mats)

    filt_shape = jax.ShapeDtypeStruct((4, sample_count, state_count), f32)
    state_shape = jax.ShapeDtypeStruct((sample_count, state_count), f32)

    kron_shape = jax.ShapeDtypeStruct((128, 128), f32)
    kron = in_vmem(call(kron_kernel, "kron", kron_shape, [SMEM])(site_trans))
    kron, start = lax.optimization_barrier((kron, start))
    dmas = [pltpu.SemaphoreType.DMA((4, 4))]
    shapes = (mats_shape, filt_shape, state_shape)
    trans, filtered, sent = call(
        forward_first_kernel, "forward_first", shapes, [VMEM] * 3 + [HBM], dmas
    )(start, near_in, far_in, in_hbm(trans_rows))
    trans = flip(in_vmem(trans), "flip_trans")
    for hop in range(1, groups):
        state = lax.ppermute(sent, "chip", [(hop - 1, hop)])
        kernel = functools.partial(forward_kernel, hop)
        filtered, sent = call(kernel, "forward", shapes[1:], [VMEM] * 5, (), {4: 0})(
            state, near_in, far_in, trans, filtered
        )

    predicted = call(predict_kernel, "predict", filt_shape, [VMEM, VMEM])(kron, filtered)
    smooth_rows, predicted = lax.optimization_barrier((smooth_rows, predicted))
    smooth, smoothed, sent = call(
        backward_first_kernel, "backward_first", shapes, [VMEM] * 2 + [HBM], dmas
    )(filtered, predicted, in_hbm(smooth_rows))
    smooth = flip(in_vmem(smooth), "flip_smooth")
    for hop in range(groups - 2, -1, -1):
        state = lax.ppermute(sent, "chip", [(hop + 1, hop)])
        kernel = functools.partial(backward_kernel, hop)
        smoothed, sent = call(kernel, "backward", shapes[1:], [VMEM] * 5, (), {4: 0})(
            state, filtered, predicted, smooth, smoothed
        )
    out_shape = jax.ShapeDtypeStruct(prior_path.shape, f32)
    return call(finish_kernel, "finish", out_shape, [VMEM, VMEM])(prior_path, smoothed)


def solution(mesh):
    times, cycle, samples = mesh.devices.shape
    by_chip = jax.sharding.Mesh(
        mesh.devices.reshape(times // 2, 2, cycle, samples), ("chip", "core", "blk", "samp")
    )
    time = ("chip", "core")
    placed = (
        P(time, "samp", "blk"),
        P(time, "blk"),
        P(time, "blk"),
        P(time, "samp", "blk"),
        P("blk", None, None),
        P("blk"),
        P("samp", "blk"),
        P(time, "blk", "samp"),
        P(time, "blk", "samp"),
        P(time, "blk", "samp"),
        P(),
    )
    return jax.shard_map(
        on_device, mesh=by_chip, in_specs=placed, out_specs=P(time, "samp", "blk"), check_vma=False
    )
```

```python
import functools
import jax
import jax.numpy as jnp
from jax import lax
from jax.experimental import pallas as pl
from jax.experimental.pallas import tpu as pltpu
from jax.sharding import PartitionSpec as P

highest = lax.Precision.HIGHEST
bf16, f32 = jnp.bfloat16, jnp.float32
ROWS_BY_ROWS = (((1,), (1,)), ((), ()))
VMEM_LIMIT = 12 * 1024 * 1024
CHUNK = 256


def ring(count, step):
    return [(i, (i + step) % count) for i in range(count)]


def swapped(count):
    return [(i, i ^ 1) for i in range(count)]


def all_blocks(value, axis):
    count = lax.axis_size(axis)
    copies = jnp.broadcast_to(value[None], (count,) + value.shape)
    return lax.all_to_all(copies, axis, 0, 0, tiled=True)


def noise_rim(noise_draw, rim=16):
    cycle, local_sites = lax.axis_size("blk"), noise_draw.shape[2]
    before = lax.ppermute(noise_draw[:, :, local_sites - rim :], "blk", ring(cycle, 1))
    after = lax.ppermute(noise_draw[:, :, :rim], "blk", ring(cycle, -1))
    return jnp.concatenate([before, noise_draw, after], axis=2)


def noise_mixer(wend_blocks, block_cols):
    block_sites = wend_blocks.shape[1]
    local_blocks = block_cols.shape[0] // 4
    cycle = lax.axis_size("blk")
    pair_rows = jnp.arange(local_blocks * 4, dtype=jnp.int32) // 4
    first_block = lax.axis_index("blk") * local_blocks
    offset = (block_cols - first_block - pair_rows + 2) % (local_blocks * cycle)
    chooser = (
        (pair_rows + offset)[:, None] == jnp.arange(local_blocks + 4, dtype=jnp.int32)[None, :]
    ).astype(f32)
    blocks = wend_blocks.reshape(local_blocks, 4, block_sites, block_sites)
    chooser = chooser.reshape(local_blocks, 4, local_blocks + 4)
    mixer = jnp.sum(chooser[:, :, :, None, None] * blocks[:, :, None, :, :], axis=1)
    return mixer.transpose(1, 3, 0, 2).reshape(
        (local_blocks + 4) * block_sites, local_blocks * block_sites
    )


def split_rows(value):
    high = value.astype(bf16)
    low = (value - high.astype(f32)).astype(bf16)
    return jnp.concatenate([high, low], axis=0)


def joined_rows(value):
    rows = value.shape[0] // 2
    return value[:rows] + value[rows:]


def start_pack(rows_ref, mats_ref, sems, order):
    steps, started = rows_ref.shape[2], {}
    for turn in order:
        started[turn] = []
        for part in range(sems.shape[1]):
            size = rows_ref.shape[1] // sems.shape[1]
            blocks = pl.ds(part * size, size)
            copy = pltpu.make_async_copy(
                rows_ref.at[turn // steps, blocks, turn % steps],
                mats_ref.at[turn, blocks],
                sems.at[turn, part],
            )
            copy.start()
            started[turn].append(copy)
    return started


def apply_rows(mats, turn, value, store):
    count, rows, _ = mats.shape[1:]
    terms = split_rows(value)
    for k in range(0, count, 2):
        block = jnp.concatenate([mats[turn, k], mats[turn, k + 1]], axis=0)
        part = lax.dot_general(terms, block, ROWS_BY_ROWS, preferred_element_type=f32)
        store(slice(k * rows, (k + 2) * rows), joined_rows(part))


def in_chunks(ref):
    return [slice(k, k + CHUNK) for k in range(0, ref.shape[-1], CHUNK)]


def apply_columns(flipped, turn, values):
    terms = [split_rows(value) for value in values]
    chunks = in_chunks(flipped)
    return [
        joined_rows(
            sum(
                jnp.dot(term, flipped[turn, rows, columns], preferred_element_type=f32)
                for term, rows in zip(terms, chunks)
            )
        )
        for columns in chunks
    ]


def flip_step(mats_ref, turn, out_ref):
    rows = mats_ref.shape[2]
    for k in range(0, mats_ref.shape[1], 2):
        block = jnp.concatenate([mats_ref[turn, k], mats_ref[turn, k + 1]], axis=0)
        for j in range(0, block.shape[1], 256):
            out_ref[turn, j : j + 256, k * rows : (k + 2) * rows] = block[:, j : j + 256].T


def flip_kernel(mats_ref, out_ref):
    def step(turn, carry):
        flip_step(mats_ref, turn, out_ref)
        return carry

    lax.fori_loop(0, mats_ref.shape[0], step, 0)


def pack_flip_kernel(rows_ref, sent_ref, out_ref, mats_ref, sems):
    copies = start_pack(rows_ref, mats_ref, sems, range(4))
    for turn in range(4):
        for copy in copies[turn]:
            copy.wait()
        flip_step(mats_ref, turn, out_ref)


def forward_step(apply, mats, turn, near_in, far_in, filt_ref, sent_ref):
    is_near = turn // 2 == lax.axis_index("core")

    def store(columns, part):
        at = lax.rem(turn, 2)
        added = jnp.where(is_near, near_in[at, :, columns], far_in[at, :, columns])
        filt_ref[turn, :, columns] = part + added

    apply(mats, turn, sent_ref[...], store)
    sent_ref[...] = filt_ref[turn]


def forward_first_kernel(state_ref, near_in, far_in, rows_ref, mats_ref, filt_ref, sent_ref, sems):
    copies = start_pack(rows_ref, mats_ref, sems, range(4))
    sent_ref[...] = state_ref[...]
    for turn in range(4):
        for copy in copies[turn]:
            copy.wait()

        @pl.when(lax.axis_index("chip") == 0)
        def _():
            at = jnp.int32(turn)
            forward_step(apply_rows, mats_ref, at, near_in, far_in, filt_ref, sent_ref)


def forward_kernel(hop, state_ref, near_in, far_in, mats, held_ref, filt_ref, sent_ref=None):
    @pl.when(lax.axis_index("chip") == hop)
    def _():
        chunks = in_chunks(state_ref)
        state = [state_ref[:, columns] for columns in chunks]
        first = lax.axis_index("core") == 0
        for turn in range(4):
            parts = apply_columns(mats, turn, state)
            for n, columns in enumerate(chunks):
                inputs = (near_in[turn % 2, :, columns], far_in[turn % 2, :, columns])
                state[n] = parts[n] + jnp.where(first, *(inputs if turn < 2 else inputs[::-1]))
                filt_ref[turn, :, columns] = state[n]
                if turn == 3 and sent_ref is not None:
                    sent_ref[:, columns] = state[n]


def backward_step(apply, mats, turn, filt_ref, pred_ref, out_ref, sent_ref):
    def store(columns, part):
        out_ref[turn, :, columns] = filt_ref[turn, :, columns] + part

    apply(mats, turn, sent_ref[...] - pred_ref[turn], store)
    sent_ref[...] = out_ref[turn]


def backward_first_kernel(filt_ref, pred_ref, rows_ref, out_ref, sent_ref, mats_ref, sems):
    @pl.when(lax.axis_index("chip") == lax.axis_size("chip") - 1)
    def _():
        copies = start_pack(rows_ref, mats_ref, sems, (2, 1, 0))
        out_ref[3] = filt_ref[3]
        sent_ref[...] = filt_ref[3]
        for turn in (2, 1, 0):
            for copy in copies[turn]:
                copy.wait()
            at = jnp.int32(turn)
            backward_step(apply_rows, mats_ref, at, filt_ref, pred_ref, out_ref, sent_ref)


def backward_kernel(hop, state_ref, filt_ref, pred_ref, mats, held_ref, out_ref, sent_ref=None):
    @pl.when(lax.axis_index("chip") == hop)
    def _():
        chunks = in_chunks(state_ref)
        state = [state_ref[:, columns] for columns in chunks]
        for turn in range(3, -1, -1):
            change = [state[n] - pred_ref[turn, :, columns] for n, columns in enumerate(chunks)]
            parts = apply_columns(mats, turn, change)
            for n, columns in enumerate(chunks):
                state[n] = filt_ref[turn, :, columns] + parts[n]
                out_ref[turn, :, columns] = state[n]
                if turn == 0 and sent_ref is not None:
                    sent_ref[:, columns] = state[n]


def finish_kernel(prior_ref, smooth_ref, out_ref):
    width = out_ref.shape[2]
    columns = pl.ds(pl.multiple_of(lax.axis_index("blk") * width, 128), width)
    for step in range(2):
        out_ref[step] = prior_ref[step] + smooth_ref[lax.axis_index("core") * 2 + step, :, columns]


def kron_kernel(site_ref, out_ref):
    row = lax.broadcasted_iota(jnp.int32, out_ref.shape, 0)
    column = lax.broadcasted_iota(jnp.int32, out_ref.shape, 1)
    same_site = row // 4 == column // 4
    kron = jnp.zeros(out_ref.shape, f32)
    for i in range(4):
        for j in range(4):
            here = same_site & (row % 4 == i) & (column % 4 == j)
            kron = jnp.where(here, site_ref[i, j], kron)
    out_ref[...] = kron


def predict_kernel(kron_ref, filt_ref, out_ref):
    steps, samples, states = filt_ref.shape
    width = kron_ref.shape[0]
    for k in range(0, states, width):
        rows = filt_ref[:, :, k : k + width].reshape(steps * samples, width)
        moved = lax.dot_general(
            rows, kron_ref[...], ROWS_BY_ROWS, precision=highest, preferred_element_type=f32
        )
        out_ref[:, :, k : k + width] = moved.reshape(steps, samples, width)


SMEM = pl.BlockSpec(memory_space=pltpu.SMEM)
VMEM = pl.BlockSpec(memory_space=pltpu.VMEM)
HBM = pl.BlockSpec(memory_space=pltpu.HBM)


def call(kernel, name, shapes, specs, scratch=(), aliases=None):
    return pl.pallas_call(
        kernel,
        out_shape=shapes,
        in_specs=specs,
        out_specs=jax.tree.map(lambda _: VMEM, shapes),
        scratch_shapes=list(scratch),
        input_output_aliases=aliases or {},
        compiler_params=pltpu.CompilerParams(vmem_limit_bytes=VMEM_LIMIT),
        name=name,
    )


def in_hbm(value):
    return pltpu.with_memory_space_constraint(value, pltpu.HBM)


def in_vmem(value):
    return pltpu.with_memory_space_constraint(value, pltpu.VMEM)


def on_device(
    prior_path,
    observed,
    obs_mask,
    noise_draw,
    wend_blocks,
    block_cols,
    start_mean,
    trans_mats,
    gain_mats,
    smooth_mats,
    site_trans,
):
    cycle, groups = lax.axis_size("blk"), lax.axis_size("chip")
    step_count, sample_count, local_sites = noise_draw.shape
    block_sites = wend_blocks.shape[1]
    state_count = trans_mats.shape[1] * cycle

    mats_shape = jax.ShapeDtypeStruct((4, cycle, trans_mats.shape[1], state_count), bf16)

    def all_rows(mats):
        whole = lax.all_gather(mats, "samp", axis=2, tiled=True)
        rows = lax.all_gather(whole, ("core", "blk"), axis=0)
        return rows.reshape((2, cycle) + rows.shape[1:])

    def flip(mats, name):
        shape = jax.ShapeDtypeStruct((4, state_count, state_count), bf16)
        return in_vmem(call(flip_kernel, name, shape, [VMEM])(mats))

    trans_rows = all_rows(trans_mats)

    widened, mixer = noise_rim(noise_draw), noise_mixer(wend_blocks, block_cols)
    obs_noise = jnp.einsum("tsl,lm->tsm", widened, mixer, precision=highest)
    first_comp = prior_path.reshape(step_count, sample_count, local_sites, 4)[:, :, :, 0]
    seen_mask = jnp.repeat(obs_mask.astype(f32), block_sites, axis=1)
    residual = seen_mask[:, None, :] * (observed[:, None, :] - first_comp - obs_noise)
    all_resid = all_blocks(residual, "blk").transpose(1, 2, 0, 3)
    all_resid = all_resid.reshape(step_count, sample_count, local_sites * cycle)
    gain = lax.all_gather(gain_mats, "samp", axis=2, tiled=True)
    inputs = jnp.einsum("tij,tsj->tsi", gain, all_resid, precision=highest)
    gathered = all_blocks(jnp.concatenate([inputs, start_mean[None]], axis=0), "blk")
    gathered = gathered.transpose(1, 2, 0, 3).reshape(step_count + 1, sample_count, state_count)
    near_in, start = gathered[:step_count], gathered[step_count]
    far_in = lax.ppermute(near_in, "core", swapped(2))
    trans_rows, near_in = lax.optimization_barrier((trans_rows, near_in))

    smooth_mats, _ = lax.optimization_barrier((smooth_mats, all_resid))
    smooth_rows = all_rows(smooth_mats)

    filt_shape = jax.ShapeDtypeStruct((4, sample_count, state_count), f32)
    state_shape = jax.ShapeDtypeStruct((sample_count, state_count), f32)

    kron_shape = jax.ShapeDtypeStruct((128, 128), f32)
    kron = in_vmem(call(kron_kernel, "kron", kron_shape, [SMEM])(site_trans))
    kron, start = lax.optimization_barrier((kron, start))
    dmas = [pltpu.SemaphoreType.DMA((4, 4))]
    shapes = (mats_shape, filt_shape, state_shape)
    trans, filtered, *sent = call(
        forward_first_kernel, "forward_first", shapes, [VMEM] * 3 + [HBM], dmas
    )(start, near_in, far_in, in_hbm(trans_rows))
    trans = flip(in_vmem(trans), "flip_trans")
    for hop in range(1, groups):
        state = lax.ppermute(sent[0], "chip", [(hop - 1, hop)])
        kernel = functools.partial(forward_kernel, hop)
        made = shapes[1:] if hop < groups - 1 else shapes[1:2]
        filtered, *sent = call(kernel, "forward", made, [VMEM] * 5, (), {4: 0})(
            state, near_in, far_in, trans, filtered
        )

    predicted = call(predict_kernel, "predict", filt_shape, [VMEM, VMEM])(kron, filtered)
    smooth_rows, predicted = lax.optimization_barrier((smooth_rows, predicted))
    held = pltpu.VMEM(mats_shape.shape, bf16)
    smoothed, *sent = call(
        backward_first_kernel, "backward_first", shapes[1:], [VMEM] * 2 + [HBM], [held] + dmas
    )(filtered, predicted, in_hbm(smooth_rows))
    flipped = jax.ShapeDtypeStruct((4, state_count, state_count), bf16)
    smooth = call(pack_flip_kernel, "pack_flip", flipped, [HBM, VMEM], [held] + dmas)(
        in_hbm(smooth_rows), sent[0]
    )
    smooth = in_vmem(smooth)
    for hop in range(groups - 2, -1, -1):
        state = lax.ppermute(sent[0], "chip", [(hop + 1, hop)])
        kernel = functools.partial(backward_kernel, hop)
        made = shapes[1:] if hop > 0 else shapes[1:2]
        smoothed, *sent = call(kernel, "backward", made, [VMEM] * 5, (), {4: 0})(
            state, filtered, predicted, smooth, smoothed
        )
    out_shape = jax.ShapeDtypeStruct(prior_path.shape, f32)
    return call(finish_kernel, "finish", out_shape, [VMEM, VMEM])(prior_path, smoothed)


def solution(mesh):
    times, cycle, samples = mesh.devices.shape
    by_chip = jax.sharding.Mesh(
        mesh.devices.reshape(times // 2, 2, cycle, samples), ("chip", "core", "blk", "samp")
    )
    time = ("chip", "core")
    placed = (
        P(time, "samp", "blk"),
        P(time, "blk"),
        P(time, "blk"),
        P(time, "samp", "blk"),
        P("blk", None, None),
        P("blk"),
        P("samp", "blk"),
        P(time, "blk", "samp"),
        P(time, "blk", "samp"),
        P(time, "blk", "samp"),
        P(),
    )
    return jax.shard_map(
        on_device, mesh=by_chip, in_specs=placed, out_specs=P(time, "samp", "blk"), check_vma=False
    )
```

```python
import functools
import jax
import jax.numpy as jnp
from jax import lax
from jax.experimental import pallas as pl
from jax.experimental.pallas import tpu as pltpu
from jax.sharding import PartitionSpec as P

highest = lax.Precision.HIGHEST
bf16, f32 = jnp.bfloat16, jnp.float32
ROWS_BY_ROWS = (((1,), (1,)), ((), ()))
VMEM_LIMIT = 12 * 1024 * 1024
CHUNK = 256
RING_ROWS = 32


def ring(count, step):
    return [(i, (i + step) % count) for i in range(count)]


def swapped(count):
    return [(i, i ^ 1) for i in range(count)]


def all_blocks(value, axis):
    count = lax.axis_size(axis)
    copies = jnp.broadcast_to(value[None], (count,) + value.shape)
    return lax.all_to_all(copies, axis, 0, 0, tiled=True)


def noise_rim(noise_draw, rim=16):
    cycle, local_sites = lax.axis_size("blk"), noise_draw.shape[2]
    before = lax.ppermute(noise_draw[:, :, local_sites - rim :], "blk", ring(cycle, 1))
    after = lax.ppermute(noise_draw[:, :, :rim], "blk", ring(cycle, -1))
    return jnp.concatenate([before, noise_draw, after], axis=2)


def noise_mixer(wend_blocks, block_cols):
    block_sites = wend_blocks.shape[1]
    local_blocks = block_cols.shape[0] // 4
    cycle = lax.axis_size("blk")
    pair_rows = jnp.arange(local_blocks * 4, dtype=jnp.int32) // 4
    first_block = lax.axis_index("blk") * local_blocks
    offset = (block_cols - first_block - pair_rows + 2) % (local_blocks * cycle)
    chooser = (
        (pair_rows + offset)[:, None] == jnp.arange(local_blocks + 4, dtype=jnp.int32)[None, :]
    ).astype(f32)
    blocks = wend_blocks.reshape(local_blocks, 4, block_sites, block_sites)
    chooser = chooser.reshape(local_blocks, 4, local_blocks + 4)
    mixer = jnp.sum(chooser[:, :, :, None, None] * blocks[:, :, None, :, :], axis=1)
    return mixer.transpose(1, 3, 0, 2).reshape(
        (local_blocks + 4) * block_sites, local_blocks * block_sites
    )


def split_rows(value):
    high = value.astype(bf16)
    low = (value - high.astype(f32)).astype(bf16)
    return jnp.concatenate([high, low], axis=0)


def joined_rows(value):
    rows = value.shape[0] // 2
    return value[:rows] + value[rows:]


def start_pack(rows_ref, mats_ref, sems, order):
    steps, started = rows_ref.shape[2], {}
    for turn in order:
        started[turn] = []
        for part in range(sems.shape[1]):
            size = rows_ref.shape[1] // sems.shape[1]
            blocks = pl.ds(part * size, size)
            copy = pltpu.make_async_copy(
                rows_ref.at[turn // steps, blocks, turn % steps],
                mats_ref.at[turn, blocks, pl.ds(0, rows_ref.shape[3])],
                sems.at[turn, part],
            )
            copy.start()
            started[turn].append(copy)
    return started


def apply_rows(mats, turn, value, store):
    count, rows, _ = mats.shape[1:]
    terms = split_rows(value)
    for k in range(0, count, 2):
        block = jnp.concatenate([mats[turn, k], mats[turn, k + 1]], axis=0)
        part = lax.dot_general(terms, block, ROWS_BY_ROWS, preferred_element_type=f32)
        store(slice(k * rows, (k + 2) * rows), joined_rows(part))


def in_chunks(ref):
    return [slice(k, k + CHUNK) for k in range(0, ref.shape[-1], CHUNK)]


def apply_columns(flipped, turn, values):
    terms = [split_rows(value) for value in values]
    chunks = in_chunks(flipped)
    return [
        joined_rows(
            sum(
                jnp.dot(term, flipped[turn, rows, columns], preferred_element_type=f32)
                for term, rows in zip(terms, chunks)
            )
        )
        for columns in chunks
    ]


def flip_step(mats_ref, turn, out_ref):
    rows = mats_ref.shape[2]
    for k in range(0, mats_ref.shape[1], 2):
        block = jnp.concatenate([mats_ref[turn, k], mats_ref[turn, k + 1]], axis=0)
        for j in range(0, block.shape[1], 256):
            out_ref[turn, j : j + 256, k * rows : (k + 2) * rows] = block[:, j : j + 256].T


def flip_kernel(mats_ref, out_ref):
    def step(turn, carry):
        flip_step(mats_ref, turn, out_ref)
        return carry

    lax.fori_loop(0, mats_ref.shape[0], step, 0)


def pack_flip_kernel(rows_ref, sent_ref, out_ref, mats_ref, sems):
    copies = start_pack(rows_ref, mats_ref, sems, range(4))
    for turn in range(4):
        for copy in copies[turn]:
            copy.wait()
        flip_step(mats_ref, turn, out_ref)


def forward_step(apply, mats, turn, near_in, far_in, filt_ref, sent_ref):
    is_near = turn // 2 == lax.axis_index("core")

    def store(columns, part):
        at = lax.rem(turn, 2)
        added = jnp.where(is_near, near_in[at, :, columns], far_in[at, :, columns])
        filt_ref[turn, :, columns] = part + added

    apply(mats, turn, sent_ref[...], store)
    sent_ref[...] = filt_ref[turn]


def forward_first_kernel(state_ref, near_in, far_in, rows_ref, *refs):
    shards, (mats_ref, filt_ref, sent_ref, sems, ring_sems) = refs[:-5], refs[-5:]
    blk, core, count = lax.axis_index("blk"), lax.axis_index("core"), len(refs[:-5]) // 2
    ring_copies = []
    for n, shard in enumerate(shards):
        steps, rows, _ = shard.shape
        owner = core if n < count else 1 - core
        at = lax.rem(blk - n % count + count, count)
        place = pl.ds(rows_ref.shape[3], rows)
        target = mats_ref.at[pl.ds(owner * steps, steps), at, place]
        ring_copies.append(pltpu.make_async_copy(shard, target, ring_sems.at[n]))
        ring_copies[-1].start()
    copies = start_pack(rows_ref, mats_ref, sems, range(4))
    for copy in ring_copies:
        copy.wait()
    sent_ref[...] = state_ref[...]
    for turn in range(4):
        for copy in copies[turn]:
            copy.wait()

        @pl.when(lax.axis_index("chip") == 0)
        def _():
            at = jnp.int32(turn)
            forward_step(apply_rows, mats_ref, at, near_in, far_in, filt_ref, sent_ref)


def forward_kernel(hop, state_ref, near_in, far_in, mats, held_ref, filt_ref, sent_ref=None):
    @pl.when(lax.axis_index("chip") == hop)
    def _():
        chunks = in_chunks(state_ref)
        state = [state_ref[:, columns] for columns in chunks]
        first = lax.axis_index("core") == 0
        for turn in range(4):
            parts = apply_columns(mats, turn, state)
            for n, columns in enumerate(chunks):
                inputs = (near_in[turn % 2, :, columns], far_in[turn % 2, :, columns])
                state[n] = parts[n] + jnp.where(first, *(inputs if turn < 2 else inputs[::-1]))
                filt_ref[turn, :, columns] = state[n]
                if turn == 3 and sent_ref is not None:
                    sent_ref[:, columns] = state[n]


def backward_step(apply, mats, turn, filt_ref, pred_ref, out_ref, sent_ref):
    def store(columns, part):
        out_ref[turn, :, columns] = filt_ref[turn, :, columns] + part

    apply(mats, turn, sent_ref[...] - pred_ref[turn], store)
    sent_ref[...] = out_ref[turn]


def backward_first_kernel(filt_ref, pred_ref, rows_ref, out_ref, sent_ref, mats_ref, sems):
    @pl.when(lax.axis_index("chip") == lax.axis_size("chip") - 1)
    def _():
        copies = start_pack(rows_ref, mats_ref, sems, (2, 1, 0))
        out_ref[3] = filt_ref[3]
        sent_ref[...] = filt_ref[3]
        for turn in (2, 1, 0):
            for copy in copies[turn]:
                copy.wait()
            at = jnp.int32(turn)
            backward_step(apply_rows, mats_ref, at, filt_ref, pred_ref, out_ref, sent_ref)


def backward_kernel(hop, state_ref, filt_ref, pred_ref, mats, held_ref, out_ref, sent_ref=None):
    @pl.when(lax.axis_index("chip") == hop)
    def _():
        chunks = in_chunks(state_ref)
        state = [state_ref[:, columns] for columns in chunks]
        for turn in range(3, -1, -1):
            change = [state[n] - pred_ref[turn, :, columns] for n, columns in enumerate(chunks)]
            parts = apply_columns(mats, turn, change)
            for n, columns in enumerate(chunks):
                state[n] = filt_ref[turn, :, columns] + parts[n]
                out_ref[turn, :, columns] = state[n]
                if turn == 0 and sent_ref is not None:
                    sent_ref[:, columns] = state[n]


def finish_kernel(prior_ref, smooth_ref, out_ref):
    width = out_ref.shape[2]
    columns = pl.ds(pl.multiple_of(lax.axis_index("blk") * width, 128), width)
    for step in range(2):
        out_ref[step] = prior_ref[step] + smooth_ref[lax.axis_index("core") * 2 + step, :, columns]


def kron_kernel(site_ref, out_ref):
    row = lax.broadcasted_iota(jnp.int32, out_ref.shape, 0)
    column = lax.broadcasted_iota(jnp.int32, out_ref.shape, 1)
    same_site = row // 4 == column // 4
    kron = jnp.zeros(out_ref.shape, f32)
    for i in range(4):
        for j in range(4):
            here = same_site & (row % 4 == i) & (column % 4 == j)
            kron = jnp.where(here, site_ref[i, j], kron)
    out_ref[...] = kron


def predict_kernel(kron_ref, filt_ref, out_ref):
    steps, samples, states = filt_ref.shape
    width = kron_ref.shape[0]
    for k in range(0, states, width):
        rows = filt_ref[:, :, k : k + width].reshape(steps * samples, width)
        moved = lax.dot_general(
            rows, kron_ref[...], ROWS_BY_ROWS, precision=highest, preferred_element_type=f32
        )
        out_ref[:, :, k : k + width] = moved.reshape(steps, samples, width)


SMEM = pl.BlockSpec(memory_space=pltpu.SMEM)
VMEM = pl.BlockSpec(memory_space=pltpu.VMEM)
HBM = pl.BlockSpec(memory_space=pltpu.HBM)
ANY = pl.BlockSpec(memory_space=pl.ANY)


def call(kernel, name, shapes, specs, scratch=(), aliases=None):
    return pl.pallas_call(
        kernel,
        out_shape=shapes,
        in_specs=specs,
        out_specs=jax.tree.map(lambda _: VMEM, shapes),
        scratch_shapes=list(scratch),
        input_output_aliases=aliases or {},
        compiler_params=pltpu.CompilerParams(vmem_limit_bytes=VMEM_LIMIT),
        name=name,
    )


def in_hbm(value):
    return pltpu.with_memory_space_constraint(value, pltpu.HBM)


def in_vmem(value):
    return pltpu.with_memory_space_constraint(value, pltpu.VMEM)


def on_device(
    prior_path,
    observed,
    obs_mask,
    noise_draw,
    wend_blocks,
    block_cols,
    start_mean,
    trans_mats,
    gain_mats,
    smooth_mats,
    site_trans,
):
    cycle, groups = lax.axis_size("blk"), lax.axis_size("chip")
    step_count, sample_count, local_sites = noise_draw.shape
    block_sites = wend_blocks.shape[1]
    state_count = trans_mats.shape[1] * cycle

    mats_shape = jax.ShapeDtypeStruct((4, cycle, trans_mats.shape[1], state_count), bf16)

    def whole_rows(mats):
        return lax.all_gather(mats, "samp", axis=2, tiled=True)

    def all_rows(whole):
        rows = lax.all_gather(whole, ("core", "blk"), axis=0)
        return rows.reshape((2, cycle) + rows.shape[1:])

    def flip(mats, name):
        shape = jax.ShapeDtypeStruct((4, state_count, state_count), bf16)
        return in_vmem(call(flip_kernel, name, shape, [VMEM])(mats))

    whole = whole_rows(trans_mats)
    cut = whole.shape[1] - RING_ROWS
    trans_rows = all_rows(whole[:, :cut])
    shards, back = [whole[:, cut:]], []
    for k in range(cycle // 2):
        shards.append(lax.ppermute(shards[-1], "blk", ring(cycle, 1)))
        if k < cycle // 2 - 1:
            back.append(lax.ppermute(back[-1] if back else shards[0], "blk", ring(cycle, -1)))
    shards += back[::-1]
    shards += [lax.ppermute(shard, "core", swapped(2)) for shard in shards]

    widened, mixer = noise_rim(noise_draw), noise_mixer(wend_blocks, block_cols)
    obs_noise = jnp.einsum("tsl,lm->tsm", widened, mixer, precision=highest)
    first_comp = prior_path.reshape(step_count, sample_count, local_sites, 4)[:, :, :, 0]
    seen_mask = jnp.repeat(obs_mask.astype(f32), block_sites, axis=1)
    residual = seen_mask[:, None, :] * (observed[:, None, :] - first_comp - obs_noise)
    all_resid = all_blocks(residual, "blk").transpose(1, 2, 0, 3)
    all_resid = all_resid.reshape(step_count, sample_count, local_sites * cycle)
    gain = lax.all_gather(gain_mats, "samp", axis=2, tiled=True)
    inputs = jnp.einsum("tij,tsj->tsi", gain, all_resid, precision=highest)
    gathered = all_blocks(jnp.concatenate([inputs, start_mean[None]], axis=0), "blk")
    gathered = gathered.transpose(1, 2, 0, 3).reshape(step_count + 1, sample_count, state_count)
    near_in, start = gathered[:step_count], gathered[step_count]
    far_in = lax.ppermute(near_in, "core", swapped(2))
    trans_rows, near_in = lax.optimization_barrier((trans_rows, near_in))

    smooth_mats, _ = lax.optimization_barrier((smooth_mats, all_resid))
    smooth_rows = all_rows(whole_rows(smooth_mats))

    filt_shape = jax.ShapeDtypeStruct((4, sample_count, state_count), f32)
    state_shape = jax.ShapeDtypeStruct((sample_count, state_count), f32)

    kron_shape = jax.ShapeDtypeStruct((128, 128), f32)
    kron = in_vmem(call(kron_kernel, "kron", kron_shape, [SMEM])(site_trans))
    kron, start = lax.optimization_barrier((kron, start))
    dmas = [pltpu.SemaphoreType.DMA((4, 4))]
    shapes = (mats_shape, filt_shape, state_shape)
    trans, filtered, *sent = call(
        forward_first_kernel,
        "forward_first",
        shapes,
        [VMEM] * 3 + [HBM] + [ANY] * len(shards),
        dmas + [pltpu.SemaphoreType.DMA((len(shards),))],
    )(start, near_in, far_in, in_hbm(trans_rows), *shards)
    trans = flip(in_vmem(trans), "flip_trans")
    for hop in range(1, groups):
        state = lax.ppermute(sent[0], "chip", [(hop - 1, hop)])
        kernel = functools.partial(forward_kernel, hop)
        made = shapes[1:] if hop < groups - 1 else shapes[1:2]
        filtered, *sent = call(kernel, "forward", made, [VMEM] * 5, (), {4: 0})(
            state, near_in, far_in, trans, filtered
        )

    predicted = call(predict_kernel, "predict", filt_shape, [VMEM, VMEM])(kron, filtered)
    smooth_rows, predicted = lax.optimization_barrier((smooth_rows, predicted))
    held = pltpu.VMEM(mats_shape.shape, bf16)
    smoothed, *sent = call(
        backward_first_kernel, "backward_first", shapes[1:], [VMEM] * 2 + [HBM], [held] + dmas
    )(filtered, predicted, in_hbm(smooth_rows))
    flipped = jax.ShapeDtypeStruct((4, state_count, state_count), bf16)
    smooth = call(pack_flip_kernel, "pack_flip", flipped, [HBM, VMEM], [held] + dmas)(
        in_hbm(smooth_rows), sent[0]
    )
    smooth = in_vmem(smooth)
    for hop in range(groups - 2, -1, -1):
        state = lax.ppermute(sent[0], "chip", [(hop + 1, hop)])
        kernel = functools.partial(backward_kernel, hop)
        made = shapes[1:] if hop > 0 else shapes[1:2]
        smoothed, *sent = call(kernel, "backward", made, [VMEM] * 5, (), {4: 0})(
            state, filtered, predicted, smooth, smoothed
        )
    out_shape = jax.ShapeDtypeStruct(prior_path.shape, f32)
    return call(finish_kernel, "finish", out_shape, [VMEM, VMEM])(prior_path, smoothed)


def solution(mesh):
    times, cycle, samples = mesh.devices.shape
    by_chip = jax.sharding.Mesh(
        mesh.devices.reshape(times // 2, 2, cycle, samples), ("chip", "core", "blk", "samp")
    )
    time = ("chip", "core")
    placed = (
        P(time, "samp", "blk"),
        P(time, "blk"),
        P(time, "blk"),
        P(time, "samp", "blk"),
        P("blk", None, None),
        P("blk"),
        P("samp", "blk"),
        P(time, "blk", "samp"),
        P(time, "blk", "samp"),
        P(time, "blk", "samp"),
        P(),
    )
    return jax.shard_map(
        on_device, mesh=by_chip, in_specs=placed, out_specs=P(time, "samp", "blk"), check_vma=False
    )
```
